512 devices in a mesh: trainer: 32 (over z_hi, x, y), depth: 16 (over z_lo, core).
Axes of the slice: x: 4, y: 4, z: 16 (z_hi: 2, z_lo: 8; z = z_hi * 8 + z_lo), core: 2. Of those that a mesh axis runs over, the one named last changes fastest.
Arguments:
- noise: bfloat16 [32, 64, 64, 256], P('trainer', 'depth'), may hold values from -6 to 6
- gen_weight: float32 [32, 331776], P('trainer', 'depth'), may hold values from -0.15625 to 0.15625
- gen_momentum: float32 [32, 331776], P('trainer', 'depth'), may hold values from -6 to 6
- disc_weight: bfloat16 [32, 8, 128, 64], P('trainer'), may hold values from -0.25 to 0.25
- score_weight: float32 [32, 128], P('trainer'), may hold values from -0.5 to 0.5
- pairing: int32 [32], replicated, may hold values from 0 to 31, as said below
- flags: int32 [32], replicated, may hold values from 0 to 1, as said below
Outputs:
- generated: bfloat16 [32, 64, 64, 256], P('trainer', 'depth')
- new_weight: float32 [32, 331776], P('trainer', 'depth')
- new_momentum: float32 [32, 331776], P('trainer', 'depth')
The draws below stay inside these ranges and needn't reach their ends.
Inputs may be any that keep to these rules, and one draw needn't show every extreme that they name: pairing is a perfect matching: pairing[pairing[i]] == i and pairing[i] != i for every trainer. `flags`: in every matched pair exactly one trainer has flag 1.
All inputs are finite; a program needn't handle non-finite values.
Results may differ from the reference program's by a relative error of at most 0.013.
Values may be sent and summed in bfloat16 or wider, within the bound.
No kernel may reach another device: no remote copies, remote signals or barrier semaphores. Data moves between devices by JAX's collectives and lax.ppermute only.
A program may use at most 64 MiB of HBM per device.

```python
import jax
import jax.numpy as jnp
import numpy as np
from jax import lax

C = 64
DC = 128
Y = 2
X = 128
YX = 256
TRAINERS = 32
NZ = 64
GEN_PARAMS = 331776


def pairing_helper(key):
    folded = jax.random.fold_in(key, 11)
    half = TRAINERS // 2
    rotation = jax.random.randint(jax.random.fold_in(folded, 1), (), 0, TRAINERS).astype(jnp.int32)
    rest_offsets = jnp.asarray(np.array([k for k in range(3, TRAINERS) if k != half], dtype=np.int32))
    shuffled = jax.random.permutation(jax.random.fold_in(folded, 2), rest_offsets)
    fixed_offsets = jnp.array([0, half, 1, 2], dtype=jnp.int32)
    order = (rotation + jnp.concatenate([fixed_offsets, shuffled.astype(jnp.int32)])) % TRAINERS
    order = order.astype(jnp.int32)
    firsts = order[0::2]
    seconds = order[1::2]
    partner_ids = jnp.zeros((TRAINERS,), jnp.int32).at[firsts].set(seconds).at[seconds].set(firsts)
    coin_flips = jax.random.randint(jax.random.fold_in(folded, 3), (half,), 0, 2).astype(jnp.int32)
    coin_flips = coin_flips.at[1].set(1)
    winner_flags = jnp.zeros((TRAINERS,), jnp.int32).at[firsts].set(coin_flips).at[seconds].set(1 - coin_flips)
    return (partner_ids.astype(jnp.int32), winner_flags.astype(jnp.int32))


def draw_pairing(key, part):
    return pairing_helper(key)[0]


def draw_flags(key, part):
    return pairing_helper(key)[1]


def block_scale(key, extent, cuts, smallest, largest):
    gain = 1.0
    for dim, shards_of in cuts:
        steps = jax.random.uniform(jax.random.fold_in(jax.random.fold_in(key, 6), dim), (shards_of,), jnp.float32, smallest / len(cuts), largest / len(cuts))
        gain = gain * jnp.repeat(jnp.exp(steps), extent[dim] // shards_of).reshape((-1,) + (1,) * (len(extent) - 1 - dim))
    return gain


def bell_draw(stream_key, extent, width, most, pieces=(), kind=jnp.bfloat16):
    entries = width * jax.random.normal(stream_key, extent, jnp.float32)
    if pieces:
        entries = entries * block_scale(stream_key, extent, pieces, -0.22, 0.18)
    return jnp.clip(entries, -most, most).astype(kind)


def setup_inputs(seed: int = 0) -> dict:
    keys = jax.random.split(jax.random.key(seed), 8)
    return {
        "noise": bell_draw(keys[0], (TRAINERS, NZ, C, YX), 1.0, 6.0, ((0, 32), (1, 16))),
        "gen_weight": bell_draw(keys[1], (TRAINERS, GEN_PARAMS), (27 * C) ** -0.5, 0.15625, ((0, 32), (1, 16)), jnp.float32),
        "gen_momentum": bell_draw(keys[2], (TRAINERS, GEN_PARAMS), 1.0, 6.0, ((0, 32), (1, 16)), jnp.float32),
        "disc_weight": bell_draw(keys[3], (TRAINERS, 8, DC, C), (8 * C) ** -0.5, 0.25, ((0, 32),)),
        "score_weight": bell_draw(keys[4], (TRAINERS, DC), DC ** -0.5, 0.5, ((0, 32),), jnp.float32),
        "pairing": draw_pairing(jax.random.fold_in(keys[7], 71), 0),
        "flags": draw_flags(jax.random.fold_in(keys[7], 71), 0),
    }


shift_table = [(shift_z, shift_y, shift_x) for shift_z in range(3) for shift_y in range(3) for shift_x in range(3)]
momentum_decay = 0.9
step_length = 0.01

def frame_all(volume):
    return jnp.pad(volume, ((0, 0), (1, 1), (1, 1), (1, 1)))

def convolve(volume, kernel):
    framed = frame_all(volume).astype(jnp.float32)
    planes, height, breadth = (volume.shape[1], volume.shape[2], volume.shape[3])
    summed = jnp.zeros((kernel.shape[1], planes, height, breadth), jnp.float32)
    for position, (shift_z, shift_y, shift_x) in enumerate(shift_table):
        window = framed[:, shift_z:shift_z + planes, shift_y:shift_y + height, shift_x:shift_x + breadth]
        summed = summed + jnp.einsum('oi,izyx->ozyx', kernel[position].astype(jnp.float32), window)
    return summed

def convolve_back(gradient, kernel):
    framed = frame_all(gradient).astype(jnp.float32)
    planes, height, breadth = (gradient.shape[1], gradient.shape[2], gradient.shape[3])
    summed = jnp.zeros((kernel.shape[2], planes, height, breadth), jnp.float32)
    for position, (shift_z, shift_y, shift_x) in enumerate(shift_table):
        window = framed[:, 2 - shift_z:2 - shift_z + planes, 2 - shift_y:2 - shift_y + height, 2 - shift_x:2 - shift_x + breadth]
        summed = summed + jnp.einsum('oi,ozyx->izyx', kernel[position].astype(jnp.float32), window)
    return summed

def kernel_grad(gradient, volume):
    framed = frame_all(volume).astype(jnp.float32)
    planes, height, breadth = (volume.shape[1], volume.shape[2], volume.shape[3])
    upstream = gradient.astype(jnp.float32)
    pieces_list = []
    for shift_z, shift_y, shift_x in shift_table:
        window = framed[:, shift_z:shift_z + planes, shift_y:shift_y + height, shift_x:shift_x + breadth]
        pieces_list.append(jnp.einsum('ozyx,izyx->oi', upstream, window))
    return jnp.stack(pieces_list)

def gelu_back(inputs, upstream):
    return jax.vjp(jax.nn.gelu, inputs)[1](upstream)[0]

def critic_grad(generated, disc_kernel, score_vector):
    channels, planes, height, breadth = generated.shape
    blocks = generated.reshape(channels, planes // 2, 2, height // 2, 2, breadth // 2, 2).astype(jnp.float32)
    kernel_cube = disc_kernel.reshape(2, 2, 2, disc_kernel.shape[1], channels).astype(jnp.float32)
    response = jnp.einsum('abdoc,czaybxd->ozyx', kernel_cube, blocks)
    features = jax.nn.gelu(response)
    scores = lax.optimization_barrier(jnp.sum(score_vector[:, None, None, None] * features, axis=0))
    slope = -jax.nn.sigmoid(-scores)
    upstream = gelu_back(response, slope[None] * score_vector[:, None, None, None]).astype(jnp.bfloat16)
    spread = jnp.einsum('abdoc,ozyx->czaybxd', kernel_cube, upstream.astype(jnp.float32))
    return spread.reshape(channels, planes, height, breadth)

def one_trainer(inputs):
    stored, weight_row, disc_kernel, score_vector = inputs
    planes_all, channels = (stored.shape[0], stored.shape[1])
    latent = stored.reshape(planes_all, channels, Y, X).transpose(1, 0, 2, 3)
    layers = weight_row.astype(jnp.bfloat16).reshape(3, 27, channels, channels)
    first_pre = convolve(latent, layers[0])
    first_act = jax.nn.gelu(first_pre).astype(jnp.bfloat16)
    second_pre = convolve(first_act, layers[1])
    second_act = jax.nn.gelu(second_pre).astype(jnp.bfloat16)
    third_pre = convolve(second_act, layers[2])
    output_f = jnp.tanh(third_pre)
    generated = output_f.astype(jnp.bfloat16)
    gen_grad = critic_grad(generated, disc_kernel, score_vector)
    third_grad = (gen_grad * (1.0 - output_f * output_f)).astype(jnp.bfloat16)
    grad_three = kernel_grad(third_grad, second_act)
    second_back = convolve_back(third_grad, layers[2])
    second_grad = gelu_back(second_pre, second_back).astype(jnp.bfloat16)
    grad_two = kernel_grad(second_grad, first_act)
    first_back = convolve_back(second_grad, layers[1])
    first_grad = gelu_back(first_pre, first_back).astype(jnp.bfloat16)
    grad_one = kernel_grad(first_grad, latent)
    weight_grad = jnp.concatenate([grad_one.reshape(-1), grad_two.reshape(-1), grad_three.reshape(-1)])
    generated_out = generated.transpose(1, 0, 2, 3).reshape(planes_all, channels, Y * X)
    return (generated_out, weight_grad)

def reference(noise, gen_weight, gen_momentum, disc_weight, score_weight, pairing, flags):
    keeper = (flags == 1)[:, None]
    chosen_weight = jnp.where(keeper, gen_weight, gen_weight[pairing])
    chosen_momentum = jnp.where(keeper, gen_momentum, gen_momentum[pairing])
    generated, weight_grad = lax.map(one_trainer, (noise, chosen_weight, disc_weight, score_weight))
    new_momentum = momentum_decay * chosen_momentum + weight_grad
    new_weight = chosen_weight - step_length * new_momentum
    return (generated, new_weight, new_momentum)
```

```python
import jax
import jax.numpy as jnp
from jax import lax
from jax.sharding import PartitionSpec as P

Y = 2
X = 128


momentum_decay = 0.9
step_length = 0.01


def extended(block, sides, width):
    for axis, dim in sides:
        count = lax.axis_size(axis)
        forward = [(i, i + 1) for i in range(count - 1)]
        backward = [(target, source) for source, target in forward]
        low = lax.ppermute(
            lax.slice_in_dim(block, block.shape[dim] - width, None, axis=dim), axis, forward
        )
        high = lax.ppermute(lax.slice_in_dim(block, 0, width, axis=dim), axis, backward)
        block = jnp.concatenate([low, block, high], axis=dim)
    return block


def framed_copies(padded):
    breadth = X
    cells = padded.shape[2]
    framed = jnp.pad(padded, ((0, 0), (0, 0), (breadth + 1, breadth + 1)))
    column = (jnp.arange(cells + 2 * breadth + 2, dtype=jnp.int32) - breadth - 1) % breadth
    left_copy = jnp.where(
        (column == breadth - 1)[None, None, :], jnp.zeros((), framed.dtype), framed
    )
    right_copy = jnp.where((column == 0)[None, None, :], jnp.zeros((), framed.dtype), framed)
    return (left_copy, framed, right_copy)


def stacked_window(copies, read_y, cells):
    breadth = X
    parts_list = []
    for read_x in range(3):
        begin = read_y * breadth + read_x
        parts_list.append(copies[read_x][:, :, begin : begin + cells])
    return jnp.concatenate(parts_list, axis=1)


def group_kernel(layer):
    channels = layer.shape[-1]
    cube = layer.reshape(3, 3, 3, channels, channels)
    return cube.transpose(0, 1, 3, 2, 4).reshape(3, 3, channels, 3 * channels)


def flip_kernel(layer):
    channels = layer.shape[-1]
    cube = layer.reshape(3, 3, 3, channels, channels)[::-1, ::-1, ::-1].swapaxes(3, 4)
    return cube.transpose(0, 1, 3, 2, 4).reshape(3, 3, channels, 3 * channels)


def convolve_grouped(padded, grouped):
    planes, cells = (padded.shape[0] - 2, padded.shape[2])
    copies = framed_copies(padded)
    summed = jnp.zeros((planes, grouped.shape[2], cells), jnp.float32)
    for read_y in range(3):
        window = stacked_window(copies, read_y, cells)
        for read_z in range(3):
            summed = summed + jnp.einsum(
                "oj,zjs->zos",
                grouped[read_z, read_y],
                window[read_z : read_z + planes],
                preferred_element_type=jnp.float32,
            )
    return summed


def convolve(padded, layer):
    return convolve_grouped(padded, group_kernel(layer))


def convolve_back(padded, layer):
    return convolve_grouped(padded, flip_kernel(layer))


def kernel_grad(gradient, padded):
    planes, channels_out, cells = gradient.shape
    channels_in = padded.shape[1]
    copies = framed_copies(padded)
    rows_list = []
    for read_z in range(3):
        row_list = []
        for read_y in range(3):
            window = stacked_window(copies, read_y, cells)
            row_list.append(
                jnp.einsum(
                    "zos,zjs->oj",
                    gradient,
                    window[read_z : read_z + planes],
                    preferred_element_type=jnp.float32,
                )
            )
        rows_list.append(jnp.stack(row_list))
    grouped = jnp.stack(rows_list)
    return (
        grouped.reshape(3, 3, channels_out, 3, channels_in)
        .transpose(0, 1, 3, 2, 4)
        .reshape(27, channels_out, channels_in)
    )


def gelu_back(inputs, upstream):
    return jax.vjp(jax.nn.gelu, inputs)[1](upstream)[0]


def widen_back(gradient):
    return extended(gradient, (("depth", 0),), 1)


def widen_forward(volume):
    return extended(volume, (("depth", 0),), 1)


def critic_grad(generated, disc_kernel, score_vector):
    planes, channels, cells = generated.shape
    blocks = generated.reshape(planes // 2, 2, channels, Y // 2, 2, X // 2, 2)
    kernel_cube = disc_kernel.reshape(2, 2, 2, disc_kernel.shape[1], channels)
    response = jnp.einsum(
        "abdoc,zacybxd->zoyx", kernel_cube, blocks, preferred_element_type=jnp.float32
    )
    features = jax.nn.gelu(response)
    scores = jnp.sum(score_vector[None, :, None, None] * features, axis=1)
    slope = -jax.nn.sigmoid(-scores)
    upstream = gelu_back(response, slope[:, None] * score_vector[None, :, None, None]).astype(
        jnp.bfloat16
    )
    spread = jnp.einsum(
        "abdoc,zoyx->zacybxd", kernel_cube, upstream, preferred_element_type=jnp.float32
    )
    return spread.reshape(planes, channels, cells)


def move(value, axis, target_of):
    count = lax.axis_size(axis)
    return lax.ppermute(value, axis, [(i, target_of(i)) for i in range(count)])


def fetch_partner(value, pairing):
    rank = lax.axis_index("trainer")
    half, row, col = rank // 16, (rank // 4) % 4, rank % 4
    across = move(value, "trainer", lambda i: i ^ 16)
    low = half == 0
    both = jnp.stack([jnp.where(low, value, across), jnp.where(low, across, value)])
    held = [both]
    for shift in range(1, 4):
        held.append(move(both, "trainer", lambda i: (i // 4) * 4 + (i + shift) % 4))
    held = jnp.concatenate(held)
    fetched = value
    own_source = pairing[rank]
    for shift in range(4):
        target = half * 16 + ((row + shift) % 4) * 4 + col
        source = pairing[target]
        slot = ((col - source % 4) % 4) * 2 + source // 16
        message = lax.dynamic_index_in_dim(held, slot, 0, keepdims=False)
        if shift:
            message = move(
                message, "trainer", lambda i: (i // 16) * 16 + (i + 4 * shift) % 16
            )
        here = (row - (own_source // 4) % 4) % 4 == shift
        fetched = jnp.where(here, message, fetched)
    return fetched


def gather_depth(block):
    rank = lax.axis_index("depth")
    shape = block.shape
    for mask in (8, 4, 2, 1):
        got = move(block, "depth", lambda i: i ^ mask)
        low = (rank & mask) == 0
        block = jnp.stack([jnp.where(low, block, got), jnp.where(low, got, block)])
    return block.transpose(3, 2, 1, 0, 4, 5).reshape(-1)


def scatter_depth(whole, share):
    rank = lax.axis_index("depth")
    held = whole.reshape((2, 2, 2, 2) + share)
    for axis, mask in ((3, 1), (2, 2), (1, 4), (0, 8)):
        bit = (rank // mask) % 2
        sent = lax.dynamic_index_in_dim(held, 1 - bit, axis, keepdims=False)
        kept = lax.dynamic_index_in_dim(held, bit, axis, keepdims=False)
        got = move(sent.astype(jnp.bfloat16), "depth", lambda i: i ^ mask)
        held = kept + got.astype(jnp.float32)
    return held


def on_device(noise, gen_weight, gen_momentum, disc_weight, score_weight, pairing, flags):
    share = (gen_weight.shape[1] // 128, 128)
    keeper = flags[lax.axis_index("trainer")] == 1
    own_weight = gen_weight.reshape(share)
    own_moment = gen_momentum.reshape(share)
    other_weight = fetch_partner(own_weight.astype(jnp.bfloat16), pairing)
    chosen_weight = jnp.where(keeper, own_weight, other_weight.astype(jnp.float32))
    sent_moment, chosen_weight = lax.optimization_barrier(
        (own_moment.astype(jnp.bfloat16), chosen_weight)
    )
    other_moment = fetch_partner(sent_moment, pairing)
    chosen_momentum = jnp.where(keeper, own_moment, other_moment.astype(jnp.float32))
    channels = noise.shape[2]
    layers = gather_depth(chosen_weight.astype(jnp.bfloat16)).reshape(3, 27, channels, channels)
    latent = noise[0]
    latent_pad = widen_forward(latent)
    first_pre = convolve(latent_pad, layers[0])
    first_act_pad = widen_forward(jax.nn.gelu(first_pre).astype(jnp.bfloat16))
    second_pre = convolve(first_act_pad, layers[1])
    second_act_pad = widen_forward(jax.nn.gelu(second_pre).astype(jnp.bfloat16))
    third_pre = convolve(second_act_pad, layers[2])
    output_f = jnp.tanh(third_pre)
    generated = output_f.astype(jnp.bfloat16)
    gen_grad = critic_grad(generated, disc_weight[0], score_weight[0])
    third_grad = (gen_grad * (1.0 - output_f * output_f)).astype(jnp.bfloat16)
    grad_three = kernel_grad(third_grad, second_act_pad)
    second_back = convolve_back(widen_back(third_grad), layers[2])
    second_grad = gelu_back(second_pre, second_back).astype(jnp.bfloat16)
    grad_two = kernel_grad(second_grad, first_act_pad)
    first_back = convolve_back(widen_back(second_grad), layers[1])
    first_grad = gelu_back(first_pre, first_back).astype(jnp.bfloat16)
    grad_one = kernel_grad(first_grad, latent_pad)
    local_grad = jnp.concatenate(
        [grad_one.reshape(-1), grad_two.reshape(-1), grad_three.reshape(-1)]
    )
    grad_share = scatter_depth(local_grad, share)
    new_momentum = momentum_decay * chosen_momentum + grad_share
    new_weight = chosen_weight - step_length * new_momentum
    new_momentum = new_momentum.reshape(gen_weight.shape)
    new_weight = new_weight.reshape(gen_weight.shape)
    return (generated[None], new_weight, new_momentum)


def solution(mesh):
    placed = (
        P("trainer", "depth", None, None),
        P("trainer", "depth"),
        P("trainer", "depth"),
        P("trainer", None, None, None),
        P("trainer", None),
        P(),
        P(),
    )
    return jax.shard_map(
        on_device,
        mesh=mesh,
        in_specs=placed,
        out_specs=(P("trainer", "depth", None, None), P("trainer", "depth"), P("trainer", "depth")),
        check_vma=False,
    )
```

```python
import math

import jax
import jax.numpy as jnp
from jax import lax
from jax.experimental import pallas as pl
from jax.experimental.pallas import tpu as pltpu
from jax.sharding import PartitionSpec as P

CH = 64
ROW = 128
ROWS = 162
SLABS = 16
PLANES = 4
DEPTH = 64
K_ROWS = 27 * CH // 2
FLAT_ROWS = 3 * K_ROWS
momentum_decay = 0.9
step_length = 0.01


def gelu_parts(x):
    c = math.sqrt(2.0 / math.pi)
    square = x * x
    t = jnp.tanh(c * (x + 0.044715 * (x * square)))
    half = 0.5 * (1.0 + t)
    slope = half + 0.5 * x * (1.0 - t * t) * (c * (1.0 + 3.0 * 0.044715 * square))
    return x * half, slope


def local_kernel(
    slab_ref,
    far_low,
    low,
    own,
    high,
    far_high,
    held_ref,
    got_ref,
    critic_ref,
    critic_back_ref,
    score_ref,
    out_ref,
    keep_ref,
    send_ref,
    raw,
    natural,
    forward_w,
    backward_w,
    win0,
    win1,
    win2,
    wing3,
    wing2,
    grad1,
    slope1,
    slope2,
    flat_k,
    flat,
):
    slab = slab_ref[0]
    lane = lax.broadcasted_iota(jnp.int32, (2 * CH, ROW), 1)
    lane_half = lax.broadcasted_iota(jnp.int32, (CH, ROW), 1)

    def store_window(target, index, value):
        target[index, 0:ROW, :] = jnp.where(lane == 0, 0.0, pltpu.roll(value, 1, 1)).astype(
            jnp.bfloat16
        )
        target[index, ROW : 2 * ROW, :] = value.astype(jnp.bfloat16)
        target[index, 2 * ROW : 3 * ROW, :] = jnp.where(
            lane == ROW - 1, 0.0, pltpu.roll(value, ROW - 1, 1)
        ).astype(jnp.bfloat16)

    def inside(plane, value):
        z = slab * PLANES + plane
        return jnp.where(jnp.logical_and(z >= 0, z < DEPTH), value, 0.0)

    sources = (
        [far_low[0]]
        + [low[i] for i in range(PLANES)]
        + [own[i] for i in range(PLANES)]
        + [high[i] for i in range(PLANES)]
        + [far_high[0]]
    )
    for index, plane in enumerate(sources):
        value = jnp.concatenate([plane[:, :ROW], plane[:, ROW:]], axis=0).astype(jnp.float32)
        store_window(win0, index, value)

    for block in range(SLABS):
        apart = block ^ slab
        slot = ((apart >> 1) & 1) * 4 + ((apart >> 2) & 1) * 2 + ((apart >> 3) & 1)
        piece = jnp.where(
            (apart & 1) == 1,
            got_ref[slot].astype(jnp.float32),
            held_ref[slot].astype(jnp.float32),
        )
        raw[block * ROWS : (block + 1) * ROWS, :] = piece

    for layer in range(3):
        rows = raw[layer * K_ROWS : (layer + 1) * K_ROWS, :]
        natural[pl.ds(layer * 2 * K_ROWS, K_ROWS, stride=2), :] = rows
        natural[pl.ds(layer * 2 * K_ROWS + 1, K_ROWS, stride=2), :] = pltpu.roll(rows, CH, 1)

    def kernel_at(layer, a, b, c):
        start = (layer * 27 + 9 * a + 3 * b + c) * CH
        return natural[start : start + CH, :]

    left = lane_half < CH
    for layer in range(3):
        for a in range(3):
            for c in range(3):
                middle = kernel_at(layer, a, 1, c)
                top = jnp.where(left, middle, pltpu.roll(kernel_at(layer, a, 2, c), CH, 1))
                bottom = jnp.where(left, kernel_at(layer, a, 0, c), pltpu.roll(middle, CH, 1))
                block = jnp.concatenate([top, bottom], axis=0)
                spot = (3 * a + c) * ROW
                forward_w[layer, :, spot : spot + ROW] = block.astype(jnp.bfloat16)
                if layer:
                    spot = (3 * (2 - a) + 2 - c) * ROW
                    backward_w[layer - 1, :, spot : spot + ROW] = block.T.astype(jnp.bfloat16)

    def pair_product(weights, windows, index):
        first = windows[index : index + 3].reshape(9 * ROW, ROW)
        second = windows[index + 1 : index + 4].reshape(9 * ROW, ROW)
        return jnp.dot(
            weights,
            jnp.concatenate([first, second], axis=1),
            preferred_element_type=jnp.float32,
        )

    for pair in range(6):
        pre = pair_product(forward_w[0], win0, 2 * pair)
        for side in range(2):
            plane = 2 * pair + side - 4
            value, slope = gelu_parts(pre[:, side * ROW : (side + 1) * ROW])
            if 0 <= plane < PLANES:
                slope1[plane] = slope
            store_window(win1, plane + 4, inside(plane, value))

    for pair in range(5):
        pre = pair_product(forward_w[1], win1, 2 * pair)
        for side in range(2):
            plane = 2 * pair + side - 3
            value, slope = gelu_parts(pre[:, side * ROW : (side + 1) * ROW])
            if -1 <= plane < PLANES + 1:
                slope2[plane + 1] = slope
            store_window(win2, plane + 3, inside(plane, value))

    even = (lane % 2) == 0
    for pair in range(4):
        pre = pair_product(forward_w[2], win2, 2 * pair)
        made = jnp.tanh(pre)
        parts = []
        for side in range(2):
            plane = 2 * pair + side - 2
            shown = made[:, side * ROW : (side + 1) * ROW].astype(jnp.bfloat16)
            if 0 <= plane < PLANES:
                out_ref[plane] = jnp.concatenate([shown[:CH], shown[CH:]], axis=1)
            parts.append(shown)
            parts.append(pltpu.roll(shown.astype(jnp.float32), ROW - 1, 1).astype(jnp.bfloat16))
        response = jnp.dot(
            critic_ref[...], jnp.concatenate(parts, axis=0), preferred_element_type=jnp.float32
        )
        features, slope = gelu_parts(response)
        score = jnp.sum(score_ref[...] * features, axis=0, keepdims=True)
        push = -jax.nn.sigmoid(-score)
        upstream = (slope * (push * score_ref[...])).astype(jnp.bfloat16).astype(jnp.float32)
        upstream = jnp.where(even, upstream, 0.0)
        both = jnp.concatenate(
            [upstream.astype(jnp.bfloat16), pltpu.roll(upstream, 1, 1).astype(jnp.bfloat16)],
            axis=0,
        )
        spread = jnp.dot(critic_back_ref[...], both, preferred_element_type=jnp.float32)
        for side in range(2):
            plane = 2 * pair + side - 2
            t = made[:, side * ROW : (side + 1) * ROW]
            grad = spread[side * ROW : (side + 1) * ROW] * (1.0 - t * t)
            grad = grad.astype(jnp.bfloat16).astype(jnp.float32)
            store_window(wing3, plane + 2, inside(plane, grad))

    def kernel_grad(layer, gradient, windows, offset):
        for a in range(3):
            moved = jnp.concatenate([windows[z + a + offset] for z in range(PLANES)], axis=1)
            product = lax.dot_general(
                gradient, moved, (((1,), (1,)), ((), ())), preferred_element_type=jnp.float32
            )
            for c in range(3):
                block = product[:, c * ROW : (c + 1) * ROW]
                top, bottom = block[:CH], block[CH:]
                values = (bottom, top + pltpu.roll(bottom, CH, 1), pltpu.roll(top, CH, 1))
                for b in range(3):
                    spot = 9 * a + 3 * b + c
                    flat_k[spot * CH : (spot + 1) * CH, :] = values[b]
        evens = flat_k[pl.ds(0, K_ROWS, stride=2), :]
        odds = flat_k[pl.ds(1, K_ROWS, stride=2), :]
        wide = lax.broadcasted_iota(jnp.int32, (K_ROWS, ROW), 1)
        flat[layer * K_ROWS : (layer + 1) * K_ROWS, :] = jnp.where(
            wide < CH, evens, pltpu.roll(odds, CH, 1)
        )

    def centre(windows, offset):
        return jnp.concatenate(
            [windows[z + offset, ROW : 2 * ROW, :] for z in range(PLANES)], axis=1
        )

    kernel_grad(2, centre(wing3, 2), win2, 2)
    for pair in range(3):
        back = pair_product(backward_w[1], wing3, 2 * pair)
        for side in range(2):
            plane = 2 * pair + side - 1
            grad = slope2[plane + 1] * back[:, side * ROW : (side + 1) * ROW]
            grad = grad.astype(jnp.bfloat16).astype(jnp.float32)
            store_window(wing2, plane + 1, inside(plane, grad))
    kernel_grad(1, centre(wing2, 1), win1, 3)
    for pair in range(2):
        back = pair_product(backward_w[0], wing2, 2 * pair)
        for side in range(2):
            plane = 2 * pair + side
            grad = slope1[plane] * back[:, side * ROW : (side + 1) * ROW]
            grad1[:, plane * ROW : (plane + 1) * ROW] = grad.astype(jnp.bfloat16)
    kernel_grad(0, grad1[...], win0, 4)

    for block in range(SLABS):
        apart = block ^ slab
        slot = ((apart >> 1) & 1) * 4 + ((apart >> 2) & 1) * 2 + ((apart >> 3) & 1)
        piece = flat[block * ROWS : (block + 1) * ROWS, :]

        @pl.when((apart & 1) == 1)
        def _():
            send_ref[slot] = piece.astype(jnp.bfloat16)

        @pl.when((apart & 1) == 0)
        def _():
            keep_ref[slot] = piece


def local_step(slab, pieces, held, got, critic, critic_back, score):
    bf16, f32 = jnp.bfloat16, jnp.float32
    vmem = pl.BlockSpec(memory_space=pltpu.VMEM)
    return pl.pallas_call(
        local_kernel,
        out_shape=(
            jax.ShapeDtypeStruct((PLANES, CH, 2 * ROW), bf16),
            jax.ShapeDtypeStruct((SLABS // 2, ROWS, ROW), f32),
            jax.ShapeDtypeStruct((SLABS // 2, ROWS, ROW), bf16),
        ),
        in_specs=[pl.BlockSpec(memory_space=pltpu.SMEM)] + [vmem] * 10,
        out_specs=(vmem, vmem, vmem),
        scratch_shapes=[
            pltpu.VMEM((FLAT_ROWS, ROW), f32),
            pltpu.VMEM((2 * FLAT_ROWS, ROW), f32),
            pltpu.VMEM((3, ROW, 9 * ROW), bf16),
            pltpu.VMEM((2, ROW, 9 * ROW), bf16),
            pltpu.VMEM((14, 3 * ROW, ROW), bf16),
            pltpu.VMEM((12, 3 * ROW, ROW), bf16),
            pltpu.VMEM((10, 3 * ROW, ROW), bf16),
            pltpu.VMEM((8, 3 * ROW, ROW), bf16),
            pltpu.VMEM((6, 3 * ROW, ROW), bf16),
            pltpu.VMEM((ROW, PLANES * ROW), bf16),
            pltpu.VMEM((PLANES, ROW, ROW), f32),
            pltpu.VMEM((PLANES + 2, ROW, ROW), f32),
            pltpu.VMEM((2 * K_ROWS, ROW), f32),
            pltpu.VMEM((FLAT_ROWS, ROW), f32),
        ],
        compiler_params=pltpu.CompilerParams(vmem_limit_bytes=48 << 20),
        cost_estimate=pl.CostEstimate(
            flops=6_000_000_000, bytes_accessed=4_000_000, transcendentals=1_000_000
        ),
        name="local_step",
    )(slab, *pieces, held, got, critic, critic_back, score)


def move(value, axis, target_of):
    count = lax.axis_size(axis)
    return lax.ppermute(value, axis, [(i, target_of(i)) for i in range(count)])


def fetch_partner(value, pairing):
    rank = lax.axis_index("trainer")
    half = rank // 16
    across = move(value, "trainer", lambda i: i ^ 16)
    wanted = lax.dynamic_slice_in_dim(pairing, half * 16, 16) // 16 == half
    slots = jnp.where(wanted.reshape((16,) + (1,) * value.ndim), value[None], across[None])
    groups = [list(range(16)), list(range(16, 32))]
    heard = lax.all_to_all(slots, "trainer", 0, 0, axis_index_groups=groups)
    return lax.dynamic_index_in_dim(heard, pairing[rank] % 16, 0, keepdims=False)


def gather_depth(block):
    held = block[None]
    for mask in (8, 4, 2):
        held = jnp.concatenate([held, move(held, "depth", lambda i: i ^ mask)])
    return held, move(held, "depth", lambda i: i ^ 1)


def scatter_depth(keep, send):
    keep = keep + move(send, "depth", lambda i: i ^ 1).astype(jnp.float32)
    for mask in (2, 4, 8):
        size = keep.shape[0] // 2
        send = keep[size:].astype(jnp.bfloat16)
        keep = keep[:size] + move(send, "depth", lambda i: i ^ mask).astype(jnp.float32)
    return keep[0]


def shifted(value, by):
    count = lax.axis_size("depth")
    links = [(i, i + by) for i in range(count) if 0 <= i + by < count]
    return lax.ppermute(value, "depth", links)


def critic_forms(disc):
    cube = disc.reshape(2, 2, 2, disc.shape[1], disc.shape[2])
    forward = cube.transpose(3, 0, 2, 1, 4).reshape(ROW, 8 * CH)
    backward = cube.transpose(0, 1, 4, 2, 3).reshape(4 * CH, 2 * ROW)
    return forward, backward


def on_device(noise, gen_weight, gen_momentum, disc_weight, score_weight, pairing, flags):
    keeper = flags[lax.axis_index("trainer")] == 1
    own_weight = gen_weight.reshape(ROWS, ROW)
    own_moment = gen_momentum.reshape(ROWS, ROW)
    sent = jnp.stack([own_weight, own_moment]).astype(jnp.bfloat16)
    other = fetch_partner(sent, pairing).astype(jnp.float32)
    chosen_weight = jnp.where(keeper, own_weight, other[0])
    chosen_momentum = jnp.where(keeper, own_moment, other[1])
    latent = noise[0]
    pieces = (
        shifted(latent[PLANES - 1 :], 2),
        shifted(latent, 1),
        latent,
        shifted(latent, -1),
        shifted(latent[:1], -2),
    )
    critic, critic_back = critic_forms(disc_weight[0])
    score = jnp.broadcast_to(score_weight[0][:, None], (ROW, ROW))
    held, got = gather_depth(chosen_weight.astype(jnp.bfloat16))
    slab = lax.axis_index("depth").astype(jnp.int32).reshape(1)
    generated, keep, send = local_step(slab, pieces, held, got, critic, critic_back, score)
    grad_share = scatter_depth(keep, send)
    new_momentum = momentum_decay * chosen_momentum + grad_share
    new_weight = chosen_weight - step_length * new_momentum
    return (
        generated[None],
        new_weight.reshape(gen_weight.shape),
        new_momentum.reshape(gen_weight.shape),
    )


def solution(mesh):
    placed = (
        P("trainer", "depth", None, None),
        P("trainer", "depth"),
        P("trainer", "depth"),
        P("trainer", None, None, None),
        P("trainer", None),
        P(),
        P(),
    )
    return jax.shard_map(
        on_device,
        mesh=mesh,
        in_specs=placed,
        out_specs=(P("trainer", "depth", None, None), P("trainer", "depth"), P("trainer", "depth")),
        check_vma=False,
    )
```

```python
import math

import jax
import jax.numpy as jnp
from jax import lax
from jax.experimental import pallas as pl
from jax.experimental.pallas import tpu as pltpu
from jax.sharding import PartitionSpec as P

CH = 64
ROW = 128
ROWS = 162
SLABS = 16
PLANES = 4
DEPTH = 64
K_ROWS = 27 * CH // 2
FLAT_ROWS = 3 * K_ROWS
momentum_decay = 0.9
step_length = 0.01


def gelu_parts(x):
    c = math.sqrt(2.0 / math.pi)
    square = x * x
    t = jnp.tanh(c * (x + 0.044715 * (x * square)))
    half = 0.5 * (1.0 + t)
    slope = half + 0.5 * x * (1.0 - t * t) * (c * (1.0 + 3.0 * 0.044715 * square))
    return x * half, slope


def local_kernel(
    slab_ref,
    far_low,
    low,
    own,
    high,
    far_high,
    held_ref,
    got_ref,
    critic_ref,
    critic_back_ref,
    score_ref,
    out_ref,
    keep_ref,
    send_ref,
    raw,
    natural,
    forward_w,
    backward_w,
    win0,
    win1,
    win2,
    wing3,
    wing2,
    grad1,
    slope1,
    slope2,
    flat_k,
    flat,
):
    slab = slab_ref[0]
    lane = lax.broadcasted_iota(jnp.int32, (2 * CH, ROW), 1)
    lane_half = lax.broadcasted_iota(jnp.int32, (CH, ROW), 1)

    def store_window(target, index, value):
        target[index, 0:ROW, :] = jnp.where(lane == 0, 0.0, pltpu.roll(value, 1, 1)).astype(
            jnp.bfloat16
        )
        target[index, ROW : 2 * ROW, :] = value.astype(jnp.bfloat16)
        target[index, 2 * ROW : 3 * ROW, :] = jnp.where(
            lane == ROW - 1, 0.0, pltpu.roll(value, ROW - 1, 1)
        ).astype(jnp.bfloat16)

    def inside(plane, value):
        z = slab * PLANES + plane
        return jnp.where(jnp.logical_and(z >= 0, z < DEPTH), value, 0.0)

    sources = (
        [far_low[0]]
        + [low[i] for i in range(PLANES)]
        + [own[i] for i in range(PLANES)]
        + [high[i] for i in range(PLANES)]
        + [far_high[0]]
    )
    for index, plane in enumerate(sources):
        value = jnp.concatenate([plane[:, :ROW], plane[:, ROW:]], axis=0).astype(jnp.float32)
        store_window(win0, index, value)

    for block in range(SLABS):
        apart = block ^ slab
        slot = ((apart >> 1) & 1) * 4 + ((apart >> 2) & 1) * 2 + block // 8
        piece = jnp.where(
            (apart & 1) == 1,
            got_ref[slot].astype(jnp.float32),
            held_ref[slot].astype(jnp.float32),
        )
        raw[block * ROWS : (block + 1) * ROWS, :] = piece

    for layer in range(3):
        rows = raw[layer * K_ROWS : (layer + 1) * K_ROWS, :]
        natural[pl.ds(layer * 2 * K_ROWS, K_ROWS, stride=2), :] = rows
        natural[pl.ds(layer * 2 * K_ROWS + 1, K_ROWS, stride=2), :] = pltpu.roll(rows, CH, 1)

    def kernel_at(layer, a, b, c):
        start = (layer * 27 + 9 * a + 3 * b + c) * CH
        return natural[start : start + CH, :]

    left = lane_half < CH
    for layer in range(3):
        for a in range(3):
            for c in range(3):
                middle = kernel_at(layer, a, 1, c)
                top = jnp.where(left, middle, pltpu.roll(kernel_at(layer, a, 2, c), CH, 1))
                bottom = jnp.where(left, kernel_at(layer, a, 0, c), pltpu.roll(middle, CH, 1))
                block = jnp.concatenate([top, bottom], axis=0)
                spot = (3 * a + c) * ROW
                forward_w[layer, :, spot : spot + ROW] = block.astype(jnp.bfloat16)
                if layer:
                    spot = (3 * (2 - a) + 2 - c) * ROW
                    backward_w[layer - 1, :, spot : spot + ROW] = block.T.astype(jnp.bfloat16)

    def pair_product(weights, windows, index):
        first = windows[index : index + 3].reshape(9 * ROW, ROW)
        second = windows[index + 1 : index + 4].reshape(9 * ROW, ROW)
        return jnp.dot(
            weights,
            jnp.concatenate([first, second], axis=1),
            preferred_element_type=jnp.float32,
        )

    for pair in range(6):
        pre = pair_product(forward_w[0], win0, 2 * pair)
        for side in range(2):
            plane = 2 * pair + side - 4
            value, slope = gelu_parts(pre[:, side * ROW : (side + 1) * ROW])
            if 0 <= plane < PLANES:
                slope1[plane] = slope
            store_window(win1, plane + 4, inside(plane, value))

    for pair in range(5):
        pre = pair_product(forward_w[1], win1, 2 * pair)
        for side in range(2):
            plane = 2 * pair + side - 3
            value, slope = gelu_parts(pre[:, side * ROW : (side + 1) * ROW])
            if -1 <= plane < PLANES + 1:
                slope2[plane + 1] = slope
            store_window(win2, plane + 3, inside(plane, value))

    even = (lane % 2) == 0
    for pair in range(4):
        pre = pair_product(forward_w[2], win2, 2 * pair)
        made = jnp.tanh(pre)
        parts = []
        for side in range(2):
            plane = 2 * pair + side - 2
            shown = made[:, side * ROW : (side + 1) * ROW].astype(jnp.bfloat16)
            if 0 <= plane < PLANES:
                out_ref[plane] = jnp.concatenate([shown[:CH], shown[CH:]], axis=1)
            parts.append(shown)
            parts.append(pltpu.roll(shown.astype(jnp.float32), ROW - 1, 1).astype(jnp.bfloat16))
        response = jnp.dot(
            critic_ref[...], jnp.concatenate(parts, axis=0), preferred_element_type=jnp.float32
        )
        features, slope = gelu_parts(response)
        score = jnp.sum(score_ref[...] * features, axis=0, keepdims=True)
        push = -jax.nn.sigmoid(-score)
        upstream = (slope * (push * score_ref[...])).astype(jnp.bfloat16).astype(jnp.float32)
        upstream = jnp.where(even, upstream, 0.0)
        both = jnp.concatenate(
            [upstream.astype(jnp.bfloat16), pltpu.roll(upstream, 1, 1).astype(jnp.bfloat16)],
            axis=0,
        )
        spread = jnp.dot(critic_back_ref[...], both, preferred_element_type=jnp.float32)
        for side in range(2):
            plane = 2 * pair + side - 2
            t = made[:, side * ROW : (side + 1) * ROW]
            grad = spread[side * ROW : (side + 1) * ROW] * (1.0 - t * t)
            grad = grad.astype(jnp.bfloat16).astype(jnp.float32)
            store_window(wing3, plane + 2, inside(plane, grad))

    def kernel_grad(layer, gradient, windows, offset):
        for a in range(3):
            moved = jnp.concatenate([windows[z + a + offset] for z in range(PLANES)], axis=1)
            product = lax.dot_general(
                gradient, moved, (((1,), (1,)), ((), ())), preferred_element_type=jnp.float32
            )
            for c in range(3):
                block = product[:, c * ROW : (c + 1) * ROW]
                top, bottom = block[:CH], block[CH:]
                values = (bottom, top + pltpu.roll(bottom, CH, 1), pltpu.roll(top, CH, 1))
                for b in range(3):
                    spot = 9 * a + 3 * b + c
                    flat_k[spot * CH : (spot + 1) * CH, :] = values[b]
        evens = flat_k[pl.ds(0, K_ROWS, stride=2), :]
        odds = flat_k[pl.ds(1, K_ROWS, stride=2), :]
        wide = lax.broadcasted_iota(jnp.int32, (K_ROWS, ROW), 1)
        flat[layer * K_ROWS : (layer + 1) * K_ROWS, :] = jnp.where(
            wide < CH, evens, pltpu.roll(odds, CH, 1)
        )

    def centre(windows, offset):
        return jnp.concatenate(
            [windows[z + offset, ROW : 2 * ROW, :] for z in range(PLANES)], axis=1
        )

    kernel_grad(2, centre(wing3, 2), win2, 2)
    for pair in range(3):
        back = pair_product(backward_w[1], wing3, 2 * pair)
        for side in range(2):
            plane = 2 * pair + side - 1
            grad = slope2[plane + 1] * back[:, side * ROW : (side + 1) * ROW]
            grad = grad.astype(jnp.bfloat16).astype(jnp.float32)
            store_window(wing2, plane + 1, inside(plane, grad))
    kernel_grad(1, centre(wing2, 1), win1, 3)
    for pair in range(2):
        back = pair_product(backward_w[0], wing2, 2 * pair)
        for side in range(2):
            plane = 2 * pair + side
            grad = slope1[plane] * back[:, side * ROW : (side + 1) * ROW]
            grad1[:, plane * ROW : (plane + 1) * ROW] = grad.astype(jnp.bfloat16)
    kernel_grad(0, grad1[...], win0, 4)

    for block in range(SLABS):
        apart = block ^ slab
        piece = flat[block * ROWS : (block + 1) * ROWS, :]

        @pl.when((apart & 1) == 1)
        def _():
            send_ref[block // 2] = piece.astype(jnp.bfloat16)

        @pl.when((apart & 1) == 0)
        def _():
            keep_ref[block // 2] = piece


def local_step(slab, pieces, held, got, critic, critic_back, score):
    bf16, f32 = jnp.bfloat16, jnp.float32
    vmem = pl.BlockSpec(memory_space=pltpu.VMEM)
    return pl.pallas_call(
        local_kernel,
        out_shape=(
            jax.ShapeDtypeStruct((PLANES, CH, 2 * ROW), bf16),
            jax.ShapeDtypeStruct((SLABS // 2, ROWS, ROW), f32),
            jax.ShapeDtypeStruct((SLABS // 2, ROWS, ROW), bf16),
        ),
        in_specs=[pl.BlockSpec(memory_space=pltpu.SMEM)] + [vmem] * 10,
        out_specs=(vmem, vmem, vmem),
        scratch_shapes=[
            pltpu.VMEM((FLAT_ROWS, ROW), f32),
            pltpu.VMEM((2 * FLAT_ROWS, ROW), f32),
            pltpu.VMEM((3, ROW, 9 * ROW), bf16),
            pltpu.VMEM((2, ROW, 9 * ROW), bf16),
            pltpu.VMEM((14, 3 * ROW, ROW), bf16),
            pltpu.VMEM((12, 3 * ROW, ROW), bf16),
            pltpu.VMEM((10, 3 * ROW, ROW), bf16),
            pltpu.VMEM((8, 3 * ROW, ROW), bf16),
            pltpu.VMEM((6, 3 * ROW, ROW), bf16),
            pltpu.VMEM((ROW, PLANES * ROW), bf16),
            pltpu.VMEM((PLANES, ROW, ROW), f32),
            pltpu.VMEM((PLANES + 2, ROW, ROW), f32),
            pltpu.VMEM((2 * K_ROWS, ROW), f32),
            pltpu.VMEM((FLAT_ROWS, ROW), f32),
        ],
        compiler_params=pltpu.CompilerParams(vmem_limit_bytes=48 << 20),
        cost_estimate=pl.CostEstimate(
            flops=6_000_000_000, bytes_accessed=4_000_000, transcendentals=1_000_000
        ),
        name="local_step",
    )(slab, *pieces, held, got, critic, critic_back, score)


def move(value, axis, target_of):
    count = lax.axis_size(axis)
    return lax.ppermute(value, axis, [(i, target_of(i)) for i in range(count)])


def plane_exchange(slots):
    groups = [list(range(16)), list(range(16, 32))]
    return lax.all_to_all(slots, "trainer", 0, 0, axis_index_groups=groups)


def source_of(trainer, pairing, flags):
    return jnp.where(flags[trainer] == 1, trainer, pairing[trainer])


def far_exchange(slots):
    depth = lax.axis_size("depth")
    groups = [
        [(t + s) * depth + d + e for s in (0, 16) for e in (0, 8)]
        for t in range(16)
        for d in range(8)
    ]
    return lax.all_to_all(slots, ("trainer", "depth"), 0, 0, axis_index_groups=groups)


def sum_depth(keep, send):
    groups = [list(range(core, 16, 2)) for core in range(2)]
    mine = keep + move(send, "depth", lambda i: i ^ 1).astype(jnp.float32)
    heard = lax.all_to_all(
        mine.astype(jnp.bfloat16), "depth", 0, 0, axis_index_groups=groups
    )
    return jnp.sum(heard.astype(jnp.float32), axis=0)


def shifted(value, by):
    count = lax.axis_size("depth")
    links = [(i, i + by) for i in range(count) if 0 <= i + by < count]
    return lax.ppermute(value, "depth", links)


def critic_forms(disc):
    cube = disc.reshape(2, 2, 2, disc.shape[1], disc.shape[2])
    forward = cube.transpose(3, 0, 2, 1, 4).reshape(ROW, 8 * CH)
    backward = cube.transpose(0, 1, 4, 2, 3).reshape(4 * CH, 2 * ROW)
    return forward, backward


def on_device(noise, gen_weight, gen_momentum, disc_weight, score_weight, pairing, flags):
    together = lax.optimization_barrier
    rank = lax.axis_index("trainer")
    slab = lax.axis_index("depth").astype(jnp.int32)
    half = rank // 16
    own_weight = gen_weight.reshape(ROWS, ROW)
    own_moment = gen_momentum.reshape(ROWS, ROW)
    sent_moment = own_moment.astype(jnp.bfloat16)
    heard = plane_exchange(
        jnp.broadcast_to(own_weight.astype(jnp.bfloat16)[None], (16, ROWS, ROW))
    )
    across = move(sent_moment, "trainer", lambda i: i ^ 16)
    latent, heard, across = together((noise[0], heard, across))
    source = source_of(rank, pairing, flags)
    other_source = source_of(rank ^ 16, pairing, flags)
    for_own = lax.dynamic_index_in_dim(heard, source % 16, 0)
    for_other = lax.dynamic_index_in_dim(heard, other_source % 16, 0)
    to_own = (jnp.arange(4) // 2 == half)[:, None, None]
    got = far_exchange(jnp.where(to_own, for_own, for_other))
    pieces = (
        shifted(latent[PLANES - 1 :], 2),
        shifted(latent, 1),
        latent,
        shifted(latent, -1),
        shifted(latent[:1], -2),
    )
    critic, critic_back = critic_forms(disc_weight[0])
    score = jnp.broadcast_to(score_weight[0][:, None], (ROW, ROW))
    got, pieces, critic, critic_back, score, across = together(
        (got, pieces, critic, critic_back, score, across)
    )
    held = lax.dynamic_slice_in_dim(got, 2 * (source // 16), 2, 0)
    other_weight = lax.dynamic_index_in_dim(held, slab // 8, 0, keepdims=False)
    wanted = lax.dynamic_slice_in_dim(pairing, half * 16, 16) // 16 == half
    heard_moment = plane_exchange(
        jnp.where(wanted[:, None, None], sent_moment[None], across[None])
    )
    for mask in (4, 2):
        held = jnp.concatenate([held, move(held, "depth", lambda i: i ^ mask)])
    near = move(held, "depth", lambda i: i ^ 1)
    generated, keep, send = local_step(
        slab.reshape(1), pieces, held, near, critic, critic_back, score
    )
    keep, send, heard_moment = together((keep, send, heard_moment))
    grad_share = sum_depth(keep, send)
    other_moment = lax.dynamic_index_in_dim(heard_moment, pairing[rank] % 16, 0, keepdims=False)
    keeper = flags[rank] == 1
    chosen_weight = jnp.where(keeper, own_weight, other_weight.astype(jnp.float32))
    chosen_momentum = jnp.where(keeper, own_moment, other_moment.astype(jnp.float32))
    new_momentum = momentum_decay * chosen_momentum + grad_share
    new_weight = chosen_weight - step_length * new_momentum
    return (
        generated[None],
        new_weight.reshape(gen_weight.shape),
        new_momentum.reshape(gen_weight.shape),
    )


def solution(mesh):
    placed = (
        P("trainer", "depth", None, None),
        P("trainer", "depth"),
        P("trainer", "depth"),
        P("trainer", None, None, None),
        P("trainer", None),
        P(),
        P(),
    )
    return jax.shard_map(
        on_device,
        mesh=mesh,
        in_specs=placed,
        out_specs=(P("trainer", "depth", None, None), P("trainer", "depth"), P("trainer", "depth")),
        check_vma=False,
    )
```

```python
import math

import jax
import jax.numpy as jnp
from jax import lax
from jax.experimental import pallas as pl
from jax.experimental.pallas import tpu as pltpu
from jax.sharding import PartitionSpec as P


CH = 64
ROW = 128
ROWS = 162
SLABS = 16
PLANES = 4
DEPTH = 64
K_ROWS = 27 * CH // 2
FLAT_ROWS = 3 * K_ROWS
momentum_decay = 0.9
step_length = 0.01


def gelu_parts(x):
    c = math.sqrt(2.0 / math.pi)
    square = x * x
    t = jnp.tanh(c * (x + 0.044715 * (x * square)))
    half = 0.5 * (1.0 + t)
    slope = half + 0.5 * x * (1.0 - t * t) * (c * (1.0 + 3.0 * 0.044715 * square))
    return x * half, slope


def local_kernel(
    slab_ref,
    far_low,
    low,
    own,
    high,
    far_high,
    held_ref,
    got_ref,
    critic_ref,
    critic_back_ref,
    score_ref,
    out_ref,
    keep_ref,
    send_ref,
    raw,
    natural,
    forward_w,
    backward_w,
    win0,
    win1,
    win2,
    wing3,
    wing2,
    grad1,
    slope1,
    slope2,
    flat_k,
    flat,
):
    slab = slab_ref[0]
    lane = lax.broadcasted_iota(jnp.int32, (2 * CH, ROW), 1)
    lane_half = lax.broadcasted_iota(jnp.int32, (CH, ROW), 1)

    def store_window(target, index, value):
        target[index, 0:ROW, :] = jnp.where(lane == 0, 0.0, pltpu.roll(value, 1, 1)).astype(
            jnp.bfloat16
        )
        target[index, ROW : 2 * ROW, :] = value.astype(jnp.bfloat16)
        target[index, 2 * ROW : 3 * ROW, :] = jnp.where(
            lane == ROW - 1, 0.0, pltpu.roll(value, ROW - 1, 1)
        ).astype(jnp.bfloat16)

    def inside(plane, value):
        z = slab * PLANES + plane
        return jnp.where(jnp.logical_and(z >= 0, z < DEPTH), value, 0.0)

    sources = (
        [far_low[0]]
        + [low[i] for i in range(PLANES)]
        + [own[i] for i in range(PLANES)]
        + [high[i] for i in range(PLANES)]
        + [far_high[0]]
    )
    for index, plane in enumerate(sources):
        value = jnp.concatenate([plane[:, :ROW], plane[:, ROW:]], axis=0).astype(jnp.float32)
        store_window(win0, index, value)

    for block in range(SLABS):
        apart = block ^ slab
        slot = ((apart >> 1) & 1) * 4 + ((apart >> 2) & 1) * 2 + block // 8
        piece = jnp.where(
            (apart & 1) == 1,
            got_ref[slot].astype(jnp.float32),
            held_ref[slot].astype(jnp.float32),
        )
        raw[block * ROWS : (block + 1) * ROWS, :] = piece

    for layer in range(3):
        rows = raw[layer * K_ROWS : (layer + 1) * K_ROWS, :]
        natural[pl.ds(layer * 2 * K_ROWS, K_ROWS, stride=2), :] = rows
        natural[pl.ds(layer * 2 * K_ROWS + 1, K_ROWS, stride=2), :] = pltpu.roll(rows, CH, 1)

    def kernel_at(layer, a, b, c):
        start = (layer * 27 + 9 * a + 3 * b + c) * CH
        return natural[start : start + CH, :]

    left = lane_half < CH
    for layer in range(3):
        for a in range(3):
            for c in range(3):
                middle = kernel_at(layer, a, 1, c)
                top = jnp.where(left, middle, pltpu.roll(kernel_at(layer, a, 2, c), CH, 1))
                bottom = jnp.where(left, kernel_at(layer, a, 0, c), pltpu.roll(middle, CH, 1))
                block = jnp.concatenate([top, bottom], axis=0)
                spot = (3 * a + c) * ROW
                forward_w[layer, :, spot : spot + ROW] = block.astype(jnp.bfloat16)
                if layer:
                    spot = (3 * (2 - a) + 2 - c) * ROW
                    backward_w[layer - 1, :, spot : spot + ROW] = block.T.astype(jnp.bfloat16)

    def pair_product(weights, windows, index):
        first = windows[index : index + 3].reshape(9 * ROW, ROW)
        second = windows[index + 1 : index + 4].reshape(9 * ROW, ROW)
        return jnp.dot(
            weights,
            jnp.concatenate([first, second], axis=1),
            preferred_element_type=jnp.float32,
        )

    for pair in range(6):
        pre = pair_product(forward_w[0], win0, 2 * pair)
        for side in range(2):
            plane = 2 * pair + side - 4
            value, slope = gelu_parts(pre[:, side * ROW : (side + 1) * ROW])
            if 0 <= plane < PLANES:
                slope1[plane] = slope
            store_window(win1, plane + 4, inside(plane, value))

    for pair in range(5):
        pre = pair_product(forward_w[1], win1, 2 * pair)
        for side in range(2):
            plane = 2 * pair + side - 3
            value, slope = gelu_parts(pre[:, side * ROW : (side + 1) * ROW])
            if -1 <= plane < PLANES + 1:
                slope2[plane + 1] = slope
            store_window(win2, plane + 3, inside(plane, value))

    even = (lane % 2) == 0
    for pair in range(4):
        pre = pair_product(forward_w[2], win2, 2 * pair)
        made = jnp.tanh(pre)
        parts = []
        for side in range(2):
            plane = 2 * pair + side - 2
            shown = made[:, side * ROW : (side + 1) * ROW].astype(jnp.bfloat16)
            if 0 <= plane < PLANES:
                out_ref[plane] = jnp.concatenate([shown[:CH], shown[CH:]], axis=1)
            parts.append(shown)
            parts.append(pltpu.roll(shown.astype(jnp.float32), ROW - 1, 1).astype(jnp.bfloat16))
        response = jnp.dot(
            critic_ref[...], jnp.concatenate(parts, axis=0), preferred_element_type=jnp.float32
        )
        features, slope = gelu_parts(response)
        score = jnp.sum(score_ref[...] * features, axis=0, keepdims=True)
        push = -jax.nn.sigmoid(-score)
        upstream = (slope * (push * score_ref[...])).astype(jnp.bfloat16).astype(jnp.float32)
        upstream = jnp.where(even, upstream, 0.0)
        both = jnp.concatenate(
            [upstream.astype(jnp.bfloat16), pltpu.roll(upstream, 1, 1).astype(jnp.bfloat16)],
            axis=0,
        )
        spread = jnp.dot(critic_back_ref[...], both, preferred_element_type=jnp.float32)
        for side in range(2):
            plane = 2 * pair + side - 2
            t = made[:, side * ROW : (side + 1) * ROW]
            grad = spread[side * ROW : (side + 1) * ROW] * (1.0 - t * t)
            grad = grad.astype(jnp.bfloat16).astype(jnp.float32)
            store_window(wing3, plane + 2, inside(plane, grad))

    def kernel_grad(layer, gradient, windows, offset):
        for a in range(3):
            moved = jnp.concatenate([windows[z + a + offset] for z in range(PLANES)], axis=1)
            product = lax.dot_general(
                gradient, moved, (((1,), (1,)), ((), ())), preferred_element_type=jnp.float32
            )
            for c in range(3):
                block = product[:, c * ROW : (c + 1) * ROW]
                top, bottom = block[:CH], block[CH:]
                values = (bottom, top + pltpu.roll(bottom, CH, 1), pltpu.roll(top, CH, 1))
                for b in range(3):
                    spot = 9 * a + 3 * b + c
                    flat_k[spot * CH : (spot + 1) * CH, :] = values[b]
        evens = flat_k[pl.ds(0, K_ROWS, stride=2), :]
        odds = flat_k[pl.ds(1, K_ROWS, stride=2), :]
        wide = lax.broadcasted_iota(jnp.int32, (K_ROWS, ROW), 1)
        flat[layer * K_ROWS : (layer + 1) * K_ROWS, :] = jnp.where(
            wide < CH, evens, pltpu.roll(odds, CH, 1)
        )

    def centre(windows, offset):
        return jnp.concatenate(
            [windows[z + offset, ROW : 2 * ROW, :] for z in range(PLANES)], axis=1
        )

    kernel_grad(2, centre(wing3, 2), win2, 2)
    for pair in range(3):
        back = pair_product(backward_w[1], wing3, 2 * pair)
        for side in range(2):
            plane = 2 * pair + side - 1
            grad = slope2[plane + 1] * back[:, side * ROW : (side + 1) * ROW]
            grad = grad.astype(jnp.bfloat16).astype(jnp.float32)
            store_window(wing2, plane + 1, inside(plane, grad))
    kernel_grad(1, centre(wing2, 1), win1, 3)
    for pair in range(2):
        back = pair_product(backward_w[0], wing2, 2 * pair)
        for side in range(2):
            plane = 2 * pair + side
            grad = slope1[plane] * back[:, side * ROW : (side + 1) * ROW]
            grad1[:, plane * ROW : (plane + 1) * ROW] = grad.astype(jnp.bfloat16)
    kernel_grad(0, grad1[...], win0, 4)

    for block in range(SLABS):
        apart = block ^ slab
        piece = flat[block * ROWS : (block + 1) * ROWS, :]

        @pl.when((apart & 1) == 1)
        def _():
            send_ref[block // 2] = piece.astype(jnp.bfloat16)

        @pl.when((apart & 1) == 0)
        def _():
            keep_ref[block // 2] = piece


def local_step(slab, pieces, held, got, critic, critic_back, score):
    bf16, f32 = jnp.bfloat16, jnp.float32
    vmem = pl.BlockSpec(memory_space=pltpu.VMEM)
    return pl.pallas_call(
        local_kernel,
        out_shape=(
            jax.ShapeDtypeStruct((PLANES, CH, 2 * ROW), bf16),
            jax.ShapeDtypeStruct((SLABS // 2, ROWS, ROW), f32),
            jax.ShapeDtypeStruct((SLABS // 2, ROWS, ROW), bf16),
        ),
        in_specs=[pl.BlockSpec(memory_space=pltpu.SMEM)] + [vmem] * 10,
        out_specs=(vmem, vmem, vmem),
        scratch_shapes=[
            pltpu.VMEM((FLAT_ROWS, ROW), f32),
            pltpu.VMEM((2 * FLAT_ROWS, ROW), f32),
            pltpu.VMEM((3, ROW, 9 * ROW), bf16),
            pltpu.VMEM((2, ROW, 9 * ROW), bf16),
            pltpu.VMEM((14, 3 * ROW, ROW), bf16),
            pltpu.VMEM((12, 3 * ROW, ROW), bf16),
            pltpu.VMEM((10, 3 * ROW, ROW), bf16),
            pltpu.VMEM((8, 3 * ROW, ROW), bf16),
            pltpu.VMEM((6, 3 * ROW, ROW), bf16),
            pltpu.VMEM((ROW, PLANES * ROW), bf16),
            pltpu.VMEM((PLANES, ROW, ROW), f32),
            pltpu.VMEM((PLANES + 2, ROW, ROW), f32),
            pltpu.VMEM((2 * K_ROWS, ROW), f32),
            pltpu.VMEM((FLAT_ROWS, ROW), f32),
        ],
        compiler_params=pltpu.CompilerParams(vmem_limit_bytes=48 << 20),
        cost_estimate=pl.CostEstimate(
            flops=6_000_000_000, bytes_accessed=4_000_000, transcendentals=1_000_000
        ),
        name="local_step",
    )(slab, *pieces, held, got, critic, critic_back, score)


def move(value, axis, target_of):
    count = lax.axis_size(axis)
    return lax.ppermute(value, axis, [(i, target_of(i)) for i in range(count)])


def plane_exchange(slots):
    groups = [list(range(16)), list(range(16, 32))]
    return lax.all_to_all(slots, "trainer", 0, 0, axis_index_groups=groups)


def source_of(trainer, pairing, flags):
    return jnp.where(flags[trainer] == 1, trainer, pairing[trainer])


def far_exchange(slots):
    depth = lax.axis_size("depth")
    groups = [
        [(t + s) * depth + d + e for s in (0, 16) for e in (0, 8)]
        for t in range(16)
        for d in range(8)
    ]
    return lax.all_to_all(slots, ("trainer", "depth"), 0, 0, axis_index_groups=groups)


def sum_depth(keep, send):
    groups = [list(range(core, 16, 2)) for core in range(2)]
    mine = keep + move(send, "depth", lambda i: i ^ 1).astype(jnp.float32)
    heard = lax.all_to_all(
        mine.astype(jnp.bfloat16), "depth", 0, 0, axis_index_groups=groups
    )
    return jnp.sum(heard.astype(jnp.float32), axis=0)


def shifted(value, by):
    count = lax.axis_size("depth")
    links = [(i, i + by) for i in range(count) if 0 <= i + by < count]
    return lax.ppermute(value, "depth", links)


def critic_forms(disc):
    cube = disc.reshape(2, 2, 2, disc.shape[1], disc.shape[2])
    forward = cube.transpose(3, 0, 2, 1, 4).reshape(ROW, 8 * CH)
    backward = cube.transpose(0, 1, 4, 2, 3).reshape(4 * CH, 2 * ROW)
    return forward, backward


def one_step(noise, gen_weight, gen_momentum, disc_weight, score_weight, pairing, flags):
    together = lax.optimization_barrier
    rank = lax.axis_index("trainer")
    slab = lax.axis_index("depth").astype(jnp.int32)
    half = rank // 16
    own_weight = gen_weight.reshape(ROWS, ROW)
    own_moment = gen_momentum.reshape(ROWS, ROW)
    latent = noise[0]
    heard = plane_exchange(jnp.broadcast_to(own_weight.astype(jnp.bfloat16)[None], (16, ROWS, ROW)))
    pieces = (
        shifted(latent[PLANES - 1 :], 2),
        shifted(latent, 1),
        latent,
        shifted(latent, -1),
        shifted(latent[:1], -2),
    )
    source = source_of(rank, pairing, flags)
    other_source = source_of(rank ^ 16, pairing, flags)
    to_own = jnp.arange(4) // 2 == half
    heard, pieces, source, other_source, to_own = together(
        (heard, pieces, source, other_source, to_own)
    )
    for_own = lax.dynamic_index_in_dim(heard, source % 16, 0)
    for_other = lax.dynamic_index_in_dim(heard, other_source % 16, 0)
    got = far_exchange(jnp.where(to_own[:, None, None], for_own, for_other))
    critic, critic_back = critic_forms(disc_weight[0])
    score = jnp.broadcast_to(score_weight[0][:, None], (ROW, ROW))
    moment_slots = jnp.broadcast_to(own_moment.astype(jnp.bfloat16)[None], (16, ROWS, ROW))
    got, critic, critic_back, score, moment_slots = together(
        (got, critic, critic_back, score, moment_slots)
    )
    held = lax.dynamic_slice_in_dim(got, 2 * (source // 16), 2, 0)
    other_weight = lax.dynamic_index_in_dim(held, slab // 8, 0, keepdims=False)
    heard_moment = plane_exchange(moment_slots)
    for mask in (4, 2):
        held = jnp.concatenate([held, move(held, "depth", lambda i: i ^ mask)])
    near = move(held, "depth", lambda i: i ^ 1)
    generated, keep, send = local_step(
        slab.reshape(1), pieces, held, near, critic, critic_back, score
    )
    keep, send, heard_moment = together((keep, send, heard_moment))
    grad_share = sum_depth(keep, send)
    moment_own = lax.dynamic_index_in_dim(heard_moment, source % 16, 0, keepdims=False)
    moment_other = lax.dynamic_index_in_dim(heard_moment, other_source % 16, 0, keepdims=False)
    moment_far = move(moment_other, "trainer", lambda i: i ^ 16)
    other_moment = jnp.where(source // 16 == half, moment_own, moment_far)
    keeper = flags[rank] == 1
    chosen_weight = jnp.where(keeper, own_weight, other_weight.astype(jnp.float32))
    chosen_momentum = jnp.where(keeper, own_moment, other_moment.astype(jnp.float32))
    new_momentum = momentum_decay * chosen_momentum + grad_share
    new_weight = chosen_weight - step_length * new_momentum
    return (
        generated[None],
        new_weight.reshape(gen_weight.shape),
        new_momentum.reshape(gen_weight.shape),
    )


def solution(mesh):
    placed = (
        P("trainer", "depth", None, None),
        P("trainer", "depth"),
        P("trainer", "depth"),
        P("trainer", None, None, None),
        P("trainer", None),
        P(),
        P(),
    )
    return jax.shard_map(
        one_step,
        mesh=mesh,
        in_specs=placed,
        out_specs=(P("trainer", "depth", None, None), P("trainer", "depth"), P("trainer", "depth")),
        check_vma=False,
    )
```

```python
import math

import jax
import jax.numpy as jnp
from jax import lax
from jax.experimental import pallas as pl
from jax.experimental.pallas import tpu as pltpu
from jax.sharding import PartitionSpec as P


CH = 64
ROW = 128
ROWS = 162
SLABS = 16
PLANES = 4
DEPTH = 64
K_ROWS = 27 * CH // 2
FLAT_ROWS = 3 * K_ROWS
momentum_decay = 0.9
step_length = 0.01


def gelu_parts(x):
    c = math.sqrt(2.0 / math.pi)
    square = x * x
    t = jnp.tanh(c * (x + 0.044715 * (x * square)))
    half = 0.5 * (1.0 + t)
    slope = half + 0.5 * x * (1.0 - t * t) * (c * (1.0 + 3.0 * 0.044715 * square))
    return x * half, slope


def local_kernel(
    slab_ref,
    far_low,
    low,
    own,
    high,
    far_high,
    held_ref,
    got_ref,
    critic_ref,
    critic_back_ref,
    score_ref,
    out_ref,
    keep_ref,
    send_ref,
    raw,
    natural,
    forward_w,
    backward_w,
    win0,
    win1,
    win2,
    wing3,
    wing2,
    grad1,
    slope1,
    slope2,
    flat_k,
    flat,
):
    slab = slab_ref[0]
    lane = lax.broadcasted_iota(jnp.int32, (2 * CH, ROW), 1)
    lane_half = lax.broadcasted_iota(jnp.int32, (CH, ROW), 1)

    def store_window(target, index, value):
        target[index, 0:ROW, :] = jnp.where(lane == 0, 0.0, pltpu.roll(value, 1, 1)).astype(
            jnp.bfloat16
        )
        target[index, ROW : 2 * ROW, :] = value.astype(jnp.bfloat16)
        target[index, 2 * ROW : 3 * ROW, :] = jnp.where(
            lane == ROW - 1, 0.0, pltpu.roll(value, ROW - 1, 1)
        ).astype(jnp.bfloat16)

    def inside(plane, value):
        z = slab * PLANES + plane
        return jnp.where(jnp.logical_and(z >= 0, z < DEPTH), value, 0.0)

    sources = (
        [far_low[0]]
        + [low[i] for i in range(PLANES)]
        + [own[i] for i in range(PLANES)]
        + [high[i] for i in range(PLANES)]
        + [far_high[0]]
    )
    for index, plane in enumerate(sources):
        value = jnp.concatenate([plane[:, :ROW], plane[:, ROW:]], axis=0).astype(jnp.float32)
        store_window(win0, index, value)

    for block in range(SLABS):
        apart = block ^ slab
        slot = ((apart >> 1) & 1) * 4 + ((apart >> 2) & 1) * 2 + block // 8
        piece = jnp.where(
            (apart & 1) == 1,
            got_ref[slot].astype(jnp.float32),
            held_ref[slot].astype(jnp.float32),
        )
        raw[block * ROWS : (block + 1) * ROWS, :] = piece

    for layer in range(3):
        rows = raw[layer * K_ROWS : (layer + 1) * K_ROWS, :]
        natural[pl.ds(layer * 2 * K_ROWS, K_ROWS, stride=2), :] = rows
        natural[pl.ds(layer * 2 * K_ROWS + 1, K_ROWS, stride=2), :] = pltpu.roll(rows, CH, 1)

    def kernel_at(layer, a, b, c):
        start = (layer * 27 + 9 * a + 3 * b + c) * CH
        return natural[start : start + CH, :]

    left = lane_half < CH
    for layer in range(3):
        for a in range(3):
            for c in range(3):
                middle = kernel_at(layer, a, 1, c)
                top = jnp.where(left, middle, pltpu.roll(kernel_at(layer, a, 2, c), CH, 1))
                bottom = jnp.where(left, kernel_at(layer, a, 0, c), pltpu.roll(middle, CH, 1))
                block = jnp.concatenate([top, bottom], axis=0)
                spot = (3 * a + c) * ROW
                forward_w[layer, :, spot : spot + ROW] = block.astype(jnp.bfloat16)
                if layer:
                    spot = (3 * (2 - a) + 2 - c) * ROW
                    backward_w[layer - 1, :, spot : spot + ROW] = block.T.astype(jnp.bfloat16)

    def pair_product(weights, windows, index):
        first = windows[index : index + 3].reshape(9 * ROW, ROW)
        second = windows[index + 1 : index + 4].reshape(9 * ROW, ROW)
        return jnp.dot(
            weights,
            jnp.concatenate([first, second], axis=1),
            preferred_element_type=jnp.float32,
        )

    for pair in range(6):
        pre = pair_product(forward_w[0], win0, 2 * pair)
        for side in range(2):
            plane = 2 * pair + side - 4
            value, slope = gelu_parts(pre[:, side * ROW : (side + 1) * ROW])
            if 0 <= plane < PLANES:
                slope1[plane] = slope
            store_window(win1, plane + 4, inside(plane, value))

    for pair in range(5):
        pre = pair_product(forward_w[1], win1, 2 * pair)
        for side in range(2):
            plane = 2 * pair + side - 3
            value, slope = gelu_parts(pre[:, side * ROW : (side + 1) * ROW])
            if -1 <= plane < PLANES + 1:
                slope2[plane + 1] = slope
            store_window(win2, plane + 3, inside(plane, value))

    even = (lane % 2) == 0
    for pair in range(4):
        pre = pair_product(forward_w[2], win2, 2 * pair)
        made = jnp.tanh(pre)
        parts = []
        for side in range(2):
            plane = 2 * pair + side - 2
            shown = made[:, side * ROW : (side + 1) * ROW].astype(jnp.bfloat16)
            if 0 <= plane < PLANES:
                out_ref[plane] = jnp.concatenate([shown[:CH], shown[CH:]], axis=1)
            parts.append(shown)
            parts.append(pltpu.roll(shown.astype(jnp.float32), ROW - 1, 1).astype(jnp.bfloat16))
        response = jnp.dot(
            critic_ref[...], jnp.concatenate(parts, axis=0), preferred_element_type=jnp.float32
        )
        features, slope = gelu_parts(response)
        score = jnp.sum(score_ref[...] * features, axis=0, keepdims=True)
        push = -jax.nn.sigmoid(-score)
        upstream = (slope * (push * score_ref[...])).astype(jnp.bfloat16).astype(jnp.float32)
        upstream = jnp.where(even, upstream, 0.0)
        both = jnp.concatenate(
            [upstream.astype(jnp.bfloat16), pltpu.roll(upstream, 1, 1).astype(jnp.bfloat16)],
            axis=0,
        )
        spread = jnp.dot(critic_back_ref[...], both, preferred_element_type=jnp.float32)
        for side in range(2):
            plane = 2 * pair + side - 2
            t = made[:, side * ROW : (side + 1) * ROW]
            grad = spread[side * ROW : (side + 1) * ROW] * (1.0 - t * t)
            grad = grad.astype(jnp.bfloat16).astype(jnp.float32)
            store_window(wing3, plane + 2, inside(plane, grad))

    def kernel_grad(layer, gradient, windows, offset):
        for a in range(3):
            moved = jnp.concatenate([windows[z + a + offset] for z in range(PLANES)], axis=1)
            product = lax.dot_general(
                gradient, moved, (((1,), (1,)), ((), ())), preferred_element_type=jnp.float32
            )
            for c in range(3):
                block = product[:, c * ROW : (c + 1) * ROW]
                top, bottom = block[:CH], block[CH:]
                values = (bottom, top + pltpu.roll(bottom, CH, 1), pltpu.roll(top, CH, 1))
                for b in range(3):
                    spot = 9 * a + 3 * b + c
                    flat_k[spot * CH : (spot + 1) * CH, :] = values[b]
        evens = flat_k[pl.ds(0, K_ROWS, stride=2), :]
        odds = flat_k[pl.ds(1, K_ROWS, stride=2), :]
        wide = lax.broadcasted_iota(jnp.int32, (K_ROWS, ROW), 1)
        flat[layer * K_ROWS : (layer + 1) * K_ROWS, :] = jnp.where(
            wide < CH, evens, pltpu.roll(odds, CH, 1)
        )

    def centre(windows, offset):
        return jnp.concatenate(
            [windows[z + offset, ROW : 2 * ROW, :] for z in range(PLANES)], axis=1
        )

    kernel_grad(2, centre(wing3, 2), win2, 2)
    for pair in range(3):
        back = pair_product(backward_w[1], wing3, 2 * pair)
        for side in range(2):
            plane = 2 * pair + side - 1
            grad = slope2[plane + 1] * back[:, side * ROW : (side + 1) * ROW]
            grad = grad.astype(jnp.bfloat16).astype(jnp.float32)
            store_window(wing2, plane + 1, inside(plane, grad))
    kernel_grad(1, centre(wing2, 1), win1, 3)
    for pair in range(2):
        back = pair_product(backward_w[0], wing2, 2 * pair)
        for side in range(2):
            plane = 2 * pair + side
            grad = slope1[plane] * back[:, side * ROW : (side + 1) * ROW]
            grad1[:, plane * ROW : (plane + 1) * ROW] = grad.astype(jnp.bfloat16)
    kernel_grad(0, grad1[...], win0, 4)

    for block in range(SLABS):
        apart = block ^ slab
        piece = flat[block * ROWS : (block + 1) * ROWS, :]

        @pl.when((apart & 1) == 1)
        def _():
            send_ref[block // 2] = piece.astype(jnp.bfloat16)

        @pl.when((apart & 1) == 0)
        def _():
            keep_ref[block // 2] = piece


def local_step(slab, pieces, held, got, critic, critic_back, score):
    bf16, f32 = jnp.bfloat16, jnp.float32
    vmem = pl.BlockSpec(memory_space=pltpu.VMEM)
    return pl.pallas_call(
        local_kernel,
        out_shape=(
            jax.ShapeDtypeStruct((PLANES, CH, 2 * ROW), bf16),
            jax.ShapeDtypeStruct((SLABS // 2, ROWS, ROW), f32),
            jax.ShapeDtypeStruct((SLABS // 2, ROWS, ROW), bf16),
        ),
        in_specs=[pl.BlockSpec(memory_space=pltpu.SMEM)] + [vmem] * 10,
        out_specs=(vmem, vmem, vmem),
        scratch_shapes=[
            pltpu.VMEM((FLAT_ROWS, ROW), f32),
            pltpu.VMEM((2 * FLAT_ROWS, ROW), f32),
            pltpu.VMEM((3, ROW, 9 * ROW), bf16),
            pltpu.VMEM((2, ROW, 9 * ROW), bf16),
            pltpu.VMEM((14, 3 * ROW, ROW), bf16),
            pltpu.VMEM((12, 3 * ROW, ROW), bf16),
            pltpu.VMEM((10, 3 * ROW, ROW), bf16),
            pltpu.VMEM((8, 3 * ROW, ROW), bf16),
            pltpu.VMEM((6, 3 * ROW, ROW), bf16),
            pltpu.VMEM((ROW, PLANES * ROW), bf16),
            pltpu.VMEM((PLANES, ROW, ROW), f32),
            pltpu.VMEM((PLANES + 2, ROW, ROW), f32),
            pltpu.VMEM((2 * K_ROWS, ROW), f32),
            pltpu.VMEM((FLAT_ROWS, ROW), f32),
        ],
        compiler_params=pltpu.CompilerParams(vmem_limit_bytes=48 << 20),
        cost_estimate=pl.CostEstimate(
            flops=6_000_000_000, bytes_accessed=4_000_000, transcendentals=1_000_000
        ),
        name="local_step",
    )(slab, *pieces, held, got, critic, critic_back, score)


def move(value, axis, target_of):
    count = lax.axis_size(axis)
    return lax.ppermute(value, axis, [(i, target_of(i)) for i in range(count)])


def plane_exchange(slots):
    groups = [list(range(16)), list(range(16, 32))]
    return lax.all_to_all(slots, "trainer", 0, 0, axis_index_groups=groups)


def source_of(trainer, pairing, flags):
    return jnp.where(flags[trainer] == 1, trainer, pairing[trainer])


def far_exchange(slots):
    depth = lax.axis_size("depth")
    groups = [
        [(t + s) * depth + d + e for s in (0, 16) for e in (0, 8)]
        for t in range(16)
        for d in range(8)
    ]
    return lax.all_to_all(slots, ("trainer", "depth"), 0, 0, axis_index_groups=groups)


def sum_depth(keep, send):
    groups = [list(range(core, 16, 2)) for core in range(2)]
    mine = keep + move(send, "depth", lambda i: i ^ 1).astype(jnp.float32)
    heard = lax.all_to_all(
        mine.astype(jnp.bfloat16), "depth", 0, 0, axis_index_groups=groups
    )
    return jnp.sum(heard.astype(jnp.float32), axis=0)


def shifted(value, by):
    count = lax.axis_size("depth")
    links = [(i, i + by) for i in range(count) if 0 <= i + by < count]
    return lax.ppermute(value, "depth", links)


def critic_forms(disc):
    cube = disc.reshape(2, 2, 2, disc.shape[1], disc.shape[2])
    forward = cube.transpose(3, 0, 2, 1, 4).reshape(ROW, 8 * CH)
    backward = cube.transpose(0, 1, 4, 2, 3).reshape(4 * CH, 2 * ROW)
    return forward, backward


def one_step(noise, gen_weight, gen_momentum, disc_weight, score_weight, pairing, flags):
    together = lax.optimization_barrier
    rank = lax.axis_index("trainer")
    slab = lax.axis_index("depth").astype(jnp.int32)
    half = rank // 16
    own_weight = gen_weight.reshape(ROWS, ROW)
    own_moment = gen_momentum.reshape(ROWS, ROW)
    sent_moment = own_moment.astype(jnp.bfloat16)
    heard = plane_exchange(jnp.broadcast_to(own_weight.astype(jnp.bfloat16)[None], (16, ROWS, ROW)))
    across = move(sent_moment, "trainer", lambda i: i ^ 16)
    source = source_of(rank, pairing, flags)
    other_source = source_of(rank ^ 16, pairing, flags)
    to_own = jnp.arange(4) // 2 == half
    wanted = lax.dynamic_slice_in_dim(pairing, half * 16, 16) // 16 == half
    latent, heard, across, source, other_source, to_own, wanted = together(
        (noise[0], heard, across, source, other_source, to_own, wanted)
    )
    for_own = lax.dynamic_index_in_dim(heard, source % 16, 0)
    for_other = lax.dynamic_index_in_dim(heard, other_source % 16, 0)
    got = far_exchange(jnp.where(to_own[:, None, None], for_own, for_other))
    low, high = shifted(latent, 1), shifted(latent, -1)
    critic, critic_back = critic_forms(disc_weight[0])
    score = jnp.broadcast_to(score_weight[0][:, None], (ROW, ROW))
    moment_slots = jnp.where(wanted[:, None, None], sent_moment[None], across[None])
    got, low, high, critic, critic_back, score, moment_slots, latent = together(
        (got, low, high, critic, critic_back, score, moment_slots, latent)
    )
    held = lax.dynamic_slice_in_dim(got, 2 * (source // 16), 2, 0)
    other_weight = lax.dynamic_index_in_dim(held, slab // 8, 0, keepdims=False)
    heard_moment = plane_exchange(moment_slots)
    held = jnp.concatenate([held, move(held, "depth", lambda i: i ^ 4)])
    held = jnp.concatenate([held, move(held, "depth", lambda i: i ^ 2)])
    far_low = shifted(latent[PLANES - 1 :], 2)
    far_high = shifted(latent[:1], -2)
    held, far_low, far_high = together((held, far_low, far_high))
    near = move(held, "depth", lambda i: i ^ 1)
    generated, keep, send = local_step(
        slab.reshape(1),
        (far_low, low, latent, high, far_high),
        held,
        near,
        critic,
        critic_back,
        score,
    )
    keep, send, heard_moment = together((keep, send, heard_moment))
    grad_share = sum_depth(keep, send)
    other_moment = lax.dynamic_index_in_dim(heard_moment, pairing[rank] % 16, 0, keepdims=False)
    keeper = flags[rank] == 1
    chosen_weight = jnp.where(keeper, own_weight, other_weight.astype(jnp.float32))
    chosen_momentum = jnp.where(keeper, own_moment, other_moment.astype(jnp.float32))
    new_momentum = momentum_decay * chosen_momentum + grad_share
    new_weight = chosen_weight - step_length * new_momentum
    return (
        generated[None],
        new_weight.reshape(gen_weight.shape),
        new_momentum.reshape(gen_weight.shape),
    )


def solution(mesh):
    placed = (
        P("trainer", "depth", None, None),
        P("trainer", "depth"),
        P("trainer", "depth"),
        P("trainer", None, None, None),
        P("trainer", None),
        P(),
        P(),
    )
    return jax.shard_map(
        one_step,
        mesh=mesh,
        in_specs=placed,
        out_specs=(P("trainer", "depth", None, None), P("trainer", "depth"), P("trainer", "depth")),
        check_vma=False,
    )
```

```python
import math

import jax
import jax.numpy as jnp
from jax import lax
from jax.experimental import pallas as pl
from jax.experimental.pallas import tpu as pltpu
from jax.sharding import PartitionSpec as P


CH = 64
ROW = 128
ROWS = 162
SECOND = 168
SLABS = 16
PLANES = 4
DEPTH = 64
K_ROWS = 27 * CH // 2
FLAT_ROWS = 3 * K_ROWS
momentum_decay = 0.9
step_length = 0.01


def gelu_parts(x):
    c = math.sqrt(2.0 / math.pi)
    square = x * x
    t = jnp.tanh(c * (x + 0.044715 * (x * square)))
    half = 0.5 * (1.0 + t)
    slope = half + 0.5 * x * (1.0 - t * t) * (c * (1.0 + 3.0 * 0.044715 * square))
    return x * half, slope


def local_kernel(
    slab_ref,
    far_low,
    low,
    own,
    high,
    far_high,
    held_ref,
    got_ref,
    critic_ref,
    critic_back_ref,
    score_ref,
    out_ref,
    keep_ref,
    send_ref,
    raw,
    natural,
    forward_w,
    backward_w,
    win0,
    win1,
    win2,
    wing3,
    wing2,
    grad1,
    slope1,
    slope2,
    flat_k,
    flat,
):
    slab = slab_ref[0]
    lane = lax.broadcasted_iota(jnp.int32, (2 * CH, ROW), 1)
    lane_half = lax.broadcasted_iota(jnp.int32, (CH, ROW), 1)

    def store_window(target, index, value):
        target[index, 0:ROW, :] = jnp.where(lane == 0, 0.0, pltpu.roll(value, 1, 1)).astype(
            jnp.bfloat16
        )
        target[index, ROW : 2 * ROW, :] = value.astype(jnp.bfloat16)
        target[index, 2 * ROW : 3 * ROW, :] = jnp.where(
            lane == ROW - 1, 0.0, pltpu.roll(value, ROW - 1, 1)
        ).astype(jnp.bfloat16)

    def inside(plane, value):
        z = slab * PLANES + plane
        return jnp.where(jnp.logical_and(z >= 0, z < DEPTH), value, 0.0)

    sources = (
        [far_low[0]]
        + [low[i] for i in range(PLANES)]
        + [own[i] for i in range(PLANES)]
        + [high[i] for i in range(PLANES)]
        + [far_high[0]]
    )
    for index, plane in enumerate(sources):
        value = jnp.concatenate([plane[:, :ROW], plane[:, ROW:]], axis=0).astype(jnp.float32)
        store_window(win0, index, value)

    for block in range(SLABS):
        apart = block ^ slab
        slot = ((apart >> 1) & 1) * 4 + ((apart >> 2) & 1) * 2 + block // 8
        piece = jnp.where(
            (apart & 1) == 1,
            got_ref[slot].astype(jnp.float32),
            held_ref[slot].astype(jnp.float32),
        )
        raw[block * ROWS : (block + 1) * ROWS, :] = piece

    for layer in range(3):
        rows = raw[layer * K_ROWS : (layer + 1) * K_ROWS, :]
        natural[pl.ds(layer * 2 * K_ROWS, K_ROWS, stride=2), :] = rows
        natural[pl.ds(layer * 2 * K_ROWS + 1, K_ROWS, stride=2), :] = pltpu.roll(rows, CH, 1)

    def kernel_at(layer, a, b, c):
        start = (layer * 27 + 9 * a + 3 * b + c) * CH
        return natural[start : start + CH, :]

    left = lane_half < CH
    for layer in range(3):
        for a in range(3):
            for c in range(3):
                middle = kernel_at(layer, a, 1, c)
                top = jnp.where(left, middle, pltpu.roll(kernel_at(layer, a, 2, c), CH, 1))
                bottom = jnp.where(left, kernel_at(layer, a, 0, c), pltpu.roll(middle, CH, 1))
                block = jnp.concatenate([top, bottom], axis=0)
                spot = (3 * a + c) * ROW
                forward_w[layer, :, spot : spot + ROW] = block.astype(jnp.bfloat16)
                if layer:
                    spot = (3 * (2 - a) + 2 - c) * ROW
                    backward_w[layer - 1, :, spot : spot + ROW] = block.T.astype(jnp.bfloat16)

    def pair_product(weights, windows, index):
        first = windows[index : index + 3].reshape(9 * ROW, ROW)
        second = windows[index + 1 : index + 4].reshape(9 * ROW, ROW)
        return jnp.dot(
            weights,
            jnp.concatenate([first, second], axis=1),
            preferred_element_type=jnp.float32,
        )

    for pair in range(6):
        pre = pair_product(forward_w[0], win0, 2 * pair)
        for side in range(2):
            plane = 2 * pair + side - 4
            value, slope = gelu_parts(pre[:, side * ROW : (side + 1) * ROW])
            if 0 <= plane < PLANES:
                slope1[plane] = slope
            store_window(win1, plane + 4, inside(plane, value))

    for pair in range(5):
        pre = pair_product(forward_w[1], win1, 2 * pair)
        for side in range(2):
            plane = 2 * pair + side - 3
            value, slope = gelu_parts(pre[:, side * ROW : (side + 1) * ROW])
            if -1 <= plane < PLANES + 1:
                slope2[plane + 1] = slope
            store_window(win2, plane + 3, inside(plane, value))

    even = (lane % 2) == 0
    for pair in range(4):
        pre = pair_product(forward_w[2], win2, 2 * pair)
        made = jnp.tanh(pre)
        parts = []
        for side in range(2):
            plane = 2 * pair + side - 2
            shown = made[:, side * ROW : (side + 1) * ROW].astype(jnp.bfloat16)
            if 0 <= plane < PLANES:
                out_ref[plane] = jnp.concatenate([shown[:CH], shown[CH:]], axis=1)
            parts.append(shown)
            parts.append(pltpu.roll(shown.astype(jnp.float32), ROW - 1, 1).astype(jnp.bfloat16))
        response = jnp.dot(
            critic_ref[...], jnp.concatenate(parts, axis=0), preferred_element_type=jnp.float32
        )
        features, slope = gelu_parts(response)
        score = jnp.sum(score_ref[...] * features, axis=0, keepdims=True)
        push = -jax.nn.sigmoid(-score)
        upstream = (slope * (push * score_ref[...])).astype(jnp.bfloat16).astype(jnp.float32)
        upstream = jnp.where(even, upstream, 0.0)
        both = jnp.concatenate(
            [upstream.astype(jnp.bfloat16), pltpu.roll(upstream, 1, 1).astype(jnp.bfloat16)],
            axis=0,
        )
        spread = jnp.dot(critic_back_ref[...], both, preferred_element_type=jnp.float32)
        for side in range(2):
            plane = 2 * pair + side - 2
            t = made[:, side * ROW : (side + 1) * ROW]
            grad = spread[side * ROW : (side + 1) * ROW] * (1.0 - t * t)
            grad = grad.astype(jnp.bfloat16).astype(jnp.float32)
            store_window(wing3, plane + 2, inside(plane, grad))

    def kernel_grad(layer, gradient, windows, offset):
        for a in range(3):
            moved = jnp.concatenate([windows[z + a + offset] for z in range(PLANES)], axis=1)
            product = lax.dot_general(
                gradient, moved, (((1,), (1,)), ((), ())), preferred_element_type=jnp.float32
            )
            for c in range(3):
                block = product[:, c * ROW : (c + 1) * ROW]
                top, bottom = block[:CH], block[CH:]
                values = (bottom, top + pltpu.roll(bottom, CH, 1), pltpu.roll(top, CH, 1))
                for b in range(3):
                    spot = 9 * a + 3 * b + c
                    flat_k[spot * CH : (spot + 1) * CH, :] = values[b]
        evens = flat_k[pl.ds(0, K_ROWS, stride=2), :]
        odds = flat_k[pl.ds(1, K_ROWS, stride=2), :]
        wide = lax.broadcasted_iota(jnp.int32, (K_ROWS, ROW), 1)
        flat[layer * K_ROWS : (layer + 1) * K_ROWS, :] = jnp.where(
            wide < CH, evens, pltpu.roll(odds, CH, 1)
        )

    def centre(windows, offset):
        return jnp.concatenate(
            [windows[z + offset, ROW : 2 * ROW, :] for z in range(PLANES)], axis=1
        )

    kernel_grad(2, centre(wing3, 2), win2, 2)
    for pair in range(3):
        back = pair_product(backward_w[1], wing3, 2 * pair)
        for side in range(2):
            plane = 2 * pair + side - 1
            grad = slope2[plane + 1] * back[:, side * ROW : (side + 1) * ROW]
            grad = grad.astype(jnp.bfloat16).astype(jnp.float32)
            store_window(wing2, plane + 1, inside(plane, grad))
    kernel_grad(1, centre(wing2, 1), win1, 3)
    for pair in range(2):
        back = pair_product(backward_w[0], wing2, 2 * pair)
        for side in range(2):
            plane = 2 * pair + side
            grad = slope1[plane] * back[:, side * ROW : (side + 1) * ROW]
            grad1[:, plane * ROW : (plane + 1) * ROW] = grad.astype(jnp.bfloat16)
    kernel_grad(0, grad1[...], win0, 4)

    for block in range(SLABS):
        apart = block ^ slab
        piece = flat[block * ROWS : (block + 1) * ROWS, :]

        @pl.when((apart & 1) == 1)
        def _():
            send_ref[block // 2] = piece.astype(jnp.bfloat16)

        @pl.when((apart & 1) == 0)
        def _():
            keep_ref[block // 2] = piece


def local_step(slab, pieces, held, got, critic, critic_back, score):
    bf16, f32 = jnp.bfloat16, jnp.float32
    vmem = pl.BlockSpec(memory_space=pltpu.VMEM)
    return pl.pallas_call(
        local_kernel,
        out_shape=(
            jax.ShapeDtypeStruct((PLANES, CH, 2 * ROW), bf16),
            jax.ShapeDtypeStruct((SLABS // 2, ROWS, ROW), f32),
            jax.ShapeDtypeStruct((SLABS // 2, ROWS, ROW), bf16),
        ),
        in_specs=[pl.BlockSpec(memory_space=pltpu.SMEM)] + [vmem] * 10,
        out_specs=(vmem, vmem, vmem),
        scratch_shapes=[
            pltpu.VMEM((FLAT_ROWS, ROW), f32),
            pltpu.VMEM((2 * FLAT_ROWS, ROW), f32),
            pltpu.VMEM((3, ROW, 9 * ROW), bf16),
            pltpu.VMEM((2, ROW, 9 * ROW), bf16),
            pltpu.VMEM((14, 3 * ROW, ROW), bf16),
            pltpu.VMEM((12, 3 * ROW, ROW), bf16),
            pltpu.VMEM((10, 3 * ROW, ROW), bf16),
            pltpu.VMEM((8, 3 * ROW, ROW), bf16),
            pltpu.VMEM((6, 3 * ROW, ROW), bf16),
            pltpu.VMEM((ROW, PLANES * ROW), bf16),
            pltpu.VMEM((PLANES, ROW, ROW), f32),
            pltpu.VMEM((PLANES + 2, ROW, ROW), f32),
            pltpu.VMEM((2 * K_ROWS, ROW), f32),
            pltpu.VMEM((FLAT_ROWS, ROW), f32),
        ],
        compiler_params=pltpu.CompilerParams(vmem_limit_bytes=48 << 20),
        cost_estimate=pl.CostEstimate(
            flops=6_000_000_000, bytes_accessed=4_000_000, transcendentals=1_000_000
        ),
        name="local_step",
    )(slab, *pieces, held, got, critic, critic_back, score)


def move(value, axis, target_of):
    count = lax.axis_size(axis)
    return lax.ppermute(value, axis, [(i, target_of(i)) for i in range(count)])


def plane_exchange(slots):
    groups = [list(range(16)), list(range(16, 32))]
    return lax.all_to_all(slots, "trainer", 0, 0, axis_index_groups=groups)


def pack_kernel(weight_ref, moment_ref, out_ref, rows):
    rows[...] = jnp.zeros(rows.shape, jnp.float32)
    for index, source in enumerate((weight_ref, moment_ref)):
        for r in range(ROWS):
            spot = index * SECOND + r
            rows[spot : spot + 1, :] = source[:, r * ROW : (r + 1) * ROW]
    packed = rows[...].astype(jnp.bfloat16)
    for slot in range(16):
        out_ref[slot] = packed


def pack_slots(weight, moment):
    vmem = pl.BlockSpec(memory_space=pltpu.VMEM)
    return pl.pallas_call(
        pack_kernel,
        out_shape=(
            jax.ShapeDtypeStruct((16, 2 * SECOND, ROW), jnp.bfloat16),
            jax.ShapeDtypeStruct((2 * SECOND, ROW), jnp.float32),
        ),
        in_specs=[vmem, vmem],
        out_specs=(vmem, vmem),
        cost_estimate=pl.CostEstimate(flops=100_000, bytes_accessed=1_500_000, transcendentals=0),
        name="pack_slots",
    )(weight, moment)


def update_kernel(info, rows, held, moment_own, across, heard, weight_ref, moment_ref, fresh):
    grad = heard[0].astype(jnp.float32)
    for member in range(1, heard.shape[0]):
        grad = grad + heard[member].astype(jnp.float32)
    keeper = info[2] == 1
    far = lax.axis_index("depth") >> 3
    other_weight = held[far].astype(jnp.float32)
    other_moment = jnp.where(
        info[1] == 1, moment_own[...].astype(jnp.float32), across[...].astype(jnp.float32)
    )
    weight = jnp.where(keeper, rows[0:ROWS, :], other_weight)
    moment = jnp.where(keeper, rows[SECOND : SECOND + ROWS, :], other_moment)
    moment = momentum_decay * moment + grad
    fresh[0] = weight - step_length * moment
    fresh[1] = moment
    for index, target in enumerate((weight_ref, moment_ref)):
        for r in range(ROWS):
            target[:, r * ROW : (r + 1) * ROW] = fresh[index, r : r + 1, :]


def update(info, rows, held, moment_own, across, heard):
    vmem = pl.BlockSpec(memory_space=pltpu.VMEM)
    flat = jax.ShapeDtypeStruct((1, ROWS * ROW), jnp.float32)
    return pl.pallas_call(
        update_kernel,
        out_shape=(flat, flat),
        in_specs=[pl.BlockSpec(memory_space=pltpu.SMEM)] + [vmem] * 5,
        out_specs=(vmem, vmem),
        scratch_shapes=[pltpu.VMEM((2, ROWS, ROW), jnp.float32)],
        cost_estimate=pl.CostEstimate(flops=500_000, bytes_accessed=1_000_000, transcendentals=0),
        name="update",
    )(info, rows, held, moment_own, across, heard)


def pick_kernel(pairing, flags, heard, slots, moment_own, moment_other, info):
    rank = lax.axis_index("trainer")
    half = rank >> 4
    across = rank ^ 16
    source = jnp.where(flags[rank] == 1, rank, pairing[rank])
    other = jnp.where(flags[across] == 1, across, pairing[across])
    for_own = heard[source & 15, 0:ROWS, :]
    for_other = heard[other & 15, 0:ROWS, :]
    for member in range(4):
        slots[member] = jnp.where(half == member // 2, for_own, for_other)
    moment_own[...] = heard[source & 15, SECOND : SECOND + ROWS, :]
    moment_other[...] = heard[other & 15, SECOND : SECOND + ROWS, :]
    info[0] = 2 * (source >> 4)
    info[1] = jnp.where((source >> 4) == half, 1, 0)
    info[2] = flags[rank]
    info[3] = half


def pick_slots(pairing, flags, heard):
    vmem = pl.BlockSpec(memory_space=pltpu.VMEM)
    smem = pl.BlockSpec(memory_space=pltpu.SMEM)
    share = jax.ShapeDtypeStruct((ROWS, ROW), jnp.bfloat16)
    return pl.pallas_call(
        pick_kernel,
        out_shape=(
            jax.ShapeDtypeStruct((4, ROWS, ROW), jnp.bfloat16),
            share,
            share,
            jax.ShapeDtypeStruct((4,), jnp.int32),
        ),
        in_specs=[smem, smem, vmem],
        out_specs=(vmem, vmem, vmem, smem),
        cost_estimate=pl.CostEstimate(flops=100_000, bytes_accessed=1_500_000, transcendentals=0),
        name="pick_slots",
    )(pairing, flags, heard)


def far_exchange(slots):
    depth = lax.axis_size("depth")
    groups = [
        [(t + s) * depth + d + e for s in (0, 16) for e in (0, 8)]
        for t in range(16)
        for d in range(8)
    ]
    return lax.all_to_all(slots, ("trainer", "depth"), 0, 0, axis_index_groups=groups)


def exchange_depth(keep, send):
    groups = [list(range(core, 16, 2)) for core in range(2)]
    mine = keep + move(send, "depth", lambda i: i ^ 1).astype(jnp.float32)
    return lax.all_to_all(
        mine.astype(jnp.bfloat16), "depth", 0, 0, axis_index_groups=groups
    )


def shifted(value, by):
    count = lax.axis_size("depth")
    links = [(i, i + by) for i in range(count) if 0 <= i + by < count]
    return lax.ppermute(value, "depth", links)


def critic_forms(disc):
    cube = disc.reshape(2, 2, 2, disc.shape[1], disc.shape[2])
    forward = cube.transpose(3, 0, 2, 1, 4).reshape(ROW, 8 * CH)
    backward = cube.transpose(0, 1, 4, 2, 3).reshape(4 * CH, 2 * ROW)
    return forward, backward


def one_step(noise, gen_weight, gen_momentum, disc_weight, score_weight, pairing, flags):
    together = lax.optimization_barrier
    slab = lax.axis_index("depth").astype(jnp.int32)
    latent = noise[0]
    packed, rows = pack_slots(gen_weight, gen_momentum)
    heard = plane_exchange(packed)
    pieces = (
        shifted(latent[PLANES - 1 :], 2),
        shifted(latent, 1),
        latent,
        shifted(latent, -1),
        shifted(latent[:1], -2),
    )
    critic, critic_back = critic_forms(disc_weight[0])
    score = jnp.broadcast_to(score_weight[0][:, None], (ROW, ROW))
    heard, pieces, critic, critic_back, score = together(
        (heard, pieces, critic, critic_back, score)
    )
    slots, moment_own, moment_other, info = pick_slots(pairing, flags, heard)
    got = far_exchange(slots)
    got, moment_other = together((got, moment_other))
    held = lax.dynamic_slice_in_dim(got, info[0], 2, 0)
    both = held
    across = move(moment_other, "trainer", lambda i: i ^ 16)
    held = jnp.concatenate([held, move(held, "depth", lambda i: i ^ 4)])
    held = jnp.concatenate([held, move(held, "depth", lambda i: i ^ 2)])
    near = move(held, "depth", lambda i: i ^ 1)
    generated, keep, send = local_step(
        slab.reshape(1), pieces, held, near, critic, critic_back, score
    )
    keep, send, across = together((keep, send, across))
    new_weight, new_momentum = update(
        info, rows, both, moment_own, across, exchange_depth(keep, send)
    )
    return generated[None], new_weight, new_momentum


def solution(mesh):
    placed = (
        P("trainer", "depth", None, None),
        P("trainer", "depth"),
        P("trainer", "depth"),
        P("trainer", None, None, None),
        P("trainer", None),
        P(),
        P(),
    )
    return jax.shard_map(
        one_step,
        mesh=mesh,
        in_specs=placed,
        out_specs=(P("trainer", "depth", None, None), P("trainer", "depth"), P("trainer", "depth")),
        check_vma=False,
    )
```

```python
import math

import jax
import jax.numpy as jnp
from jax import lax
from jax.experimental import pallas as pl
from jax.experimental.pallas import tpu as pltpu
from jax.sharding import PartitionSpec as P


CH = 64
ROW = 128
ROWS = 162
SECOND = 168
SLABS = 16
PLANES = 4
DEPTH = 64
K_ROWS = 27 * CH // 2
FLAT_ROWS = 3 * K_ROWS
momentum_decay = 0.9
step_length = 0.01


def gelu_parts(x):
    c = math.sqrt(2.0 / math.pi)
    square = x * x
    t = jnp.tanh(c * (x + 0.044715 * (x * square)))
    half = 0.5 * (1.0 + t)
    slope = half + 0.5 * x * (1.0 - t * t) * (c * (1.0 + 3.0 * 0.044715 * square))
    return x * half, slope


def local_kernel(
    slab_ref,
    far_low,
    low,
    own,
    high,
    far_high,
    held_ref,
    got_ref,
    critic_ref,
    critic_back_ref,
    score_ref,
    out_ref,
    keep_ref,
    send_ref,
    raw,
    natural,
    forward_w,
    backward_w,
    win0,
    win1,
    win2,
    wing3,
    wing2,
    grad1,
    slope1,
    slope2,
    flat_k,
    flat,
):
    slab = slab_ref[0]
    lane = lax.broadcasted_iota(jnp.int32, (2 * CH, ROW), 1)
    lane_half = lax.broadcasted_iota(jnp.int32, (CH, ROW), 1)

    def store_window(target, index, value):
        target[index, 0:ROW, :] = jnp.where(lane == 0, 0.0, pltpu.roll(value, 1, 1)).astype(
            jnp.bfloat16
        )
        target[index, ROW : 2 * ROW, :] = value.astype(jnp.bfloat16)
        target[index, 2 * ROW : 3 * ROW, :] = jnp.where(
            lane == ROW - 1, 0.0, pltpu.roll(value, ROW - 1, 1)
        ).astype(jnp.bfloat16)

    def inside(plane, value):
        z = slab * PLANES + plane
        return jnp.where(jnp.logical_and(z >= 0, z < DEPTH), value, 0.0)

    sources = (
        [far_low[0]]
        + [low[i] for i in range(PLANES)]
        + [own[i] for i in range(PLANES)]
        + [high[i] for i in range(PLANES)]
        + [far_high[0]]
    )
    for index, plane in enumerate(sources):
        value = jnp.concatenate([plane[:, :ROW], plane[:, ROW:]], axis=0).astype(jnp.float32)
        store_window(win0, index, value)

    for block in range(SLABS):
        apart = block ^ slab
        slot = ((apart >> 1) & 1) * 4 + ((apart >> 2) & 1) * 2 + block // 8
        piece = jnp.where(
            (apart & 1) == 1,
            got_ref[slot].astype(jnp.float32),
            held_ref[slot].astype(jnp.float32),
        )
        raw[block * ROWS : (block + 1) * ROWS, :] = piece

    for layer in range(3):
        rows = raw[layer * K_ROWS : (layer + 1) * K_ROWS, :]
        natural[pl.ds(layer * 2 * K_ROWS, K_ROWS, stride=2), :] = rows
        natural[pl.ds(layer * 2 * K_ROWS + 1, K_ROWS, stride=2), :] = pltpu.roll(rows, CH, 1)

    def kernel_at(layer, a, b, c):
        start = (layer * 27 + 9 * a + 3 * b + c) * CH
        return natural[start : start + CH, :]

    left = lane_half < CH
    for layer in range(3):
        for a in range(3):
            for c in range(3):
                middle = kernel_at(layer, a, 1, c)
                top = jnp.where(left, middle, pltpu.roll(kernel_at(layer, a, 2, c), CH, 1))
                bottom = jnp.where(left, kernel_at(layer, a, 0, c), pltpu.roll(middle, CH, 1))
                block = jnp.concatenate([top, bottom], axis=0)
                spot = (3 * a + c) * ROW
                forward_w[layer, :, spot : spot + ROW] = block.astype(jnp.bfloat16)
                if layer:
                    spot = (3 * (2 - a) + 2 - c) * ROW
                    backward_w[layer - 1, :, spot : spot + ROW] = block.T.astype(jnp.bfloat16)

    def pair_product(weights, windows, index):
        first = windows[index : index + 3].reshape(9 * ROW, ROW)
        second = windows[index + 1 : index + 4].reshape(9 * ROW, ROW)
        return jnp.dot(
            weights,
            jnp.concatenate([first, second], axis=1),
            preferred_element_type=jnp.float32,
        )

    for pair in range(6):
        pre = pair_product(forward_w[0], win0, 2 * pair)
        for side in range(2):
            plane = 2 * pair + side - 4
            value, slope = gelu_parts(pre[:, side * ROW : (side + 1) * ROW])
            if 0 <= plane < PLANES:
                slope1[plane] = slope
            store_window(win1, plane + 4, inside(plane, value))

    for pair in range(5):
        pre = pair_product(forward_w[1], win1, 2 * pair)
        for side in range(2):
            plane = 2 * pair + side - 3
            value, slope = gelu_parts(pre[:, side * ROW : (side + 1) * ROW])
            if -1 <= plane < PLANES + 1:
                slope2[plane + 1] = slope
            store_window(win2, plane + 3, inside(plane, value))

    even = (lane % 2) == 0
    for pair in range(4):
        pre = pair_product(forward_w[2], win2, 2 * pair)
        made = jnp.tanh(pre)
        parts = []
        for side in range(2):
            plane = 2 * pair + side - 2
            shown = made[:, side * ROW : (side + 1) * ROW].astype(jnp.bfloat16)
            if 0 <= plane < PLANES:
                out_ref[plane] = jnp.concatenate([shown[:CH], shown[CH:]], axis=1)
            parts.append(shown)
            parts.append(pltpu.roll(shown.astype(jnp.float32), ROW - 1, 1).astype(jnp.bfloat16))
        response = jnp.dot(
            critic_ref[...], jnp.concatenate(parts, axis=0), preferred_element_type=jnp.float32
        )
        features, slope = gelu_parts(response)
        score = jnp.sum(score_ref[...] * features, axis=0, keepdims=True)
        push = -jax.nn.sigmoid(-score)
        upstream = (slope * (push * score_ref[...])).astype(jnp.bfloat16).astype(jnp.float32)
        upstream = jnp.where(even, upstream, 0.0)
        both = jnp.concatenate(
            [upstream.astype(jnp.bfloat16), pltpu.roll(upstream, 1, 1).astype(jnp.bfloat16)],
            axis=0,
        )
        spread = jnp.dot(critic_back_ref[...], both, preferred_element_type=jnp.float32)
        for side in range(2):
            plane = 2 * pair + side - 2
            t = made[:, side * ROW : (side + 1) * ROW]
            grad = spread[side * ROW : (side + 1) * ROW] * (1.0 - t * t)
            grad = grad.astype(jnp.bfloat16).astype(jnp.float32)
            store_window(wing3, plane + 2, inside(plane, grad))

    def kernel_grad(layer, gradient, windows, offset):
        for a in range(3):
            moved = jnp.concatenate([windows[z + a + offset] for z in range(PLANES)], axis=1)
            product = lax.dot_general(
                gradient, moved, (((1,), (1,)), ((), ())), preferred_element_type=jnp.float32
            )
            for c in range(3):
                block = product[:, c * ROW : (c + 1) * ROW]
                top, bottom = block[:CH], block[CH:]
                values = (bottom, top + pltpu.roll(bottom, CH, 1), pltpu.roll(top, CH, 1))
                for b in range(3):
                    spot = 9 * a + 3 * b + c
                    flat_k[spot * CH : (spot + 1) * CH, :] = values[b]
        evens = flat_k[pl.ds(0, K_ROWS, stride=2), :]
        odds = flat_k[pl.ds(1, K_ROWS, stride=2), :]
        wide = lax.broadcasted_iota(jnp.int32, (K_ROWS, ROW), 1)
        flat[layer * K_ROWS : (layer + 1) * K_ROWS, :] = jnp.where(
            wide < CH, evens, pltpu.roll(odds, CH, 1)
        )

    def centre(windows, offset):
        return jnp.concatenate(
            [windows[z + offset, ROW : 2 * ROW, :] for z in range(PLANES)], axis=1
        )

    kernel_grad(2, centre(wing3, 2), win2, 2)
    for pair in range(3):
        back = pair_product(backward_w[1], wing3, 2 * pair)
        for side in range(2):
            plane = 2 * pair + side - 1
            grad = slope2[plane + 1] * back[:, side * ROW : (side + 1) * ROW]
            grad = grad.astype(jnp.bfloat16).astype(jnp.float32)
            store_window(wing2, plane + 1, inside(plane, grad))
    kernel_grad(1, centre(wing2, 1), win1, 3)
    for pair in range(2):
        back = pair_product(backward_w[0], wing2, 2 * pair)
        for side in range(2):
            plane = 2 * pair + side
            grad = slope1[plane] * back[:, side * ROW : (side + 1) * ROW]
            grad1[:, plane * ROW : (plane + 1) * ROW] = grad.astype(jnp.bfloat16)
    kernel_grad(0, grad1[...], win0, 4)

    for block in range(SLABS):
        apart = block ^ slab
        piece = flat[block * ROWS : (block + 1) * ROWS, :]

        @pl.when((apart & 1) == 1)
        def _():
            send_ref[block // 2] = piece.astype(jnp.bfloat16)

        @pl.when((apart & 1) == 0)
        def _():
            keep_ref[block // 2] = piece


def local_step(slab, pieces, held, got, critic, critic_back, score):
    bf16, f32 = jnp.bfloat16, jnp.float32
    vmem = pl.BlockSpec(memory_space=pltpu.VMEM)
    return pl.pallas_call(
        local_kernel,
        out_shape=(
            jax.ShapeDtypeStruct((PLANES, CH, 2 * ROW), bf16),
            jax.ShapeDtypeStruct((SLABS // 2, ROWS, ROW), f32),
            jax.ShapeDtypeStruct((SLABS // 2, ROWS, ROW), bf16),
        ),
        in_specs=[pl.BlockSpec(memory_space=pltpu.SMEM)] + [vmem] * 10,
        out_specs=(vmem, vmem, vmem),
        scratch_shapes=[
            pltpu.VMEM((FLAT_ROWS, ROW), f32),
            pltpu.VMEM((2 * FLAT_ROWS, ROW), f32),
            pltpu.VMEM((3, ROW, 9 * ROW), bf16),
            pltpu.VMEM((2, ROW, 9 * ROW), bf16),
            pltpu.VMEM((14, 3 * ROW, ROW), bf16),
            pltpu.VMEM((12, 3 * ROW, ROW), bf16),
            pltpu.VMEM((10, 3 * ROW, ROW), bf16),
            pltpu.VMEM((8, 3 * ROW, ROW), bf16),
            pltpu.VMEM((6, 3 * ROW, ROW), bf16),
            pltpu.VMEM((ROW, PLANES * ROW), bf16),
            pltpu.VMEM((PLANES, ROW, ROW), f32),
            pltpu.VMEM((PLANES + 2, ROW, ROW), f32),
            pltpu.VMEM((2 * K_ROWS, ROW), f32),
            pltpu.VMEM((FLAT_ROWS, ROW), f32),
        ],
        compiler_params=pltpu.CompilerParams(vmem_limit_bytes=24 << 20),
        cost_estimate=pl.CostEstimate(
            flops=6_000_000_000, bytes_accessed=4_000_000, transcendentals=1_000_000
        ),
        name="local_step",
    )(slab, *pieces, held, got, critic, critic_back, score)


def move(value, axis, target_of):
    count = lax.axis_size(axis)
    return lax.ppermute(value, axis, [(i, target_of(i)) for i in range(count)])


def plane_exchange(slots):
    groups = [list(range(16)), list(range(16, 32))]
    return lax.all_to_all(slots, "trainer", 0, 0, axis_index_groups=groups)


def pack_kernel(weight_ref, moment_ref, out_ref, rows):
    rows[...] = jnp.zeros(rows.shape, jnp.float32)
    for index, source in enumerate((weight_ref, moment_ref)):
        for r in range(ROWS):
            spot = index * SECOND + r
            rows[spot : spot + 1, :] = source[:, r * ROW : (r + 1) * ROW]
    packed = rows[...].astype(jnp.bfloat16)
    for slot in range(16):
        out_ref[slot] = packed


def pack_slots(weight, moment):
    vmem = pl.BlockSpec(memory_space=pltpu.VMEM)
    return pl.pallas_call(
        pack_kernel,
        out_shape=(
            jax.ShapeDtypeStruct((16, 2 * SECOND, ROW), jnp.bfloat16),
            jax.ShapeDtypeStruct((2 * SECOND, ROW), jnp.float32),
        ),
        in_specs=[vmem, vmem],
        out_specs=(vmem, vmem),
        cost_estimate=pl.CostEstimate(flops=100_000, bytes_accessed=1_500_000, transcendentals=0),
        compiler_params=pltpu.CompilerParams(vmem_limit_bytes=8 << 20),
        name="pack_slots",
    )(weight, moment)


def update_kernel(info, rows, held, moment_own, across, heard, weight_ref, moment_ref, fresh):
    grad = heard[0].astype(jnp.float32)
    for member in range(1, heard.shape[0]):
        grad = grad + heard[member].astype(jnp.float32)
    keeper = info[2] == 1
    far = lax.axis_index("depth") >> 3
    other_weight = held[far].astype(jnp.float32)
    other_moment = jnp.where(
        info[1] == 1, moment_own[...].astype(jnp.float32), across[...].astype(jnp.float32)
    )
    weight = jnp.where(keeper, rows[0:ROWS, :], other_weight)
    moment = jnp.where(keeper, rows[SECOND : SECOND + ROWS, :], other_moment)
    moment = momentum_decay * moment + grad
    fresh[0] = weight - step_length * moment
    fresh[1] = moment
    for index, target in enumerate((weight_ref, moment_ref)):
        for r in range(ROWS):
            target[:, r * ROW : (r + 1) * ROW] = fresh[index, r : r + 1, :]


def update(info, rows, held, moment_own, across, heard):
    vmem = pl.BlockSpec(memory_space=pltpu.VMEM)
    flat = jax.ShapeDtypeStruct((1, ROWS * ROW), jnp.float32)
    return pl.pallas_call(
        update_kernel,
        out_shape=(flat, flat),
        in_specs=[pl.BlockSpec(memory_space=pltpu.SMEM)] + [vmem] * 5,
        out_specs=(vmem, vmem),
        scratch_shapes=[pltpu.VMEM((2, ROWS, ROW), jnp.float32)],
        cost_estimate=pl.CostEstimate(flops=500_000, bytes_accessed=1_000_000, transcendentals=0),
        compiler_params=pltpu.CompilerParams(vmem_limit_bytes=8 << 20),
        name="update",
    )(info, rows, held, moment_own, across, heard)


def pick_kernel(
    pairing, flags, heard, slots, moment_own, moment_other, info, for_own, for_other, sems
):
    rank = lax.axis_index("trainer")
    half = rank >> 4
    across = rank ^ 16
    source = jnp.where(flags[rank] == 1, rank, pairing[rank])
    other = jnp.where(flags[across] == 1, across, pairing[across])
    first = pltpu.make_async_copy(heard.at[source & 15], for_own, sems.at[0])
    second = pltpu.make_async_copy(heard.at[other & 15], for_other, sems.at[1])
    first.start()
    second.start()
    info[0] = 2 * (source >> 4)
    info[1] = jnp.where((source >> 4) == half, 1, 0)
    info[2] = flags[rank]
    info[3] = half
    first.wait()
    second.wait()
    for member in range(4):
        slots[member] = jnp.where(half == member // 2, for_own[0:ROWS, :], for_other[0:ROWS, :])
    moment_own[...] = for_own[SECOND : SECOND + ROWS, :]
    moment_other[...] = for_other[SECOND : SECOND + ROWS, :]


def pick_slots(pairing, flags, heard):
    vmem = pl.BlockSpec(memory_space=pltpu.VMEM)
    smem = pl.BlockSpec(memory_space=pltpu.SMEM)
    share = jax.ShapeDtypeStruct((ROWS, ROW), jnp.bfloat16)
    return pl.pallas_call(
        pick_kernel,
        out_shape=(
            jax.ShapeDtypeStruct((4, ROWS, ROW), jnp.bfloat16),
            share,
            share,
            jax.ShapeDtypeStruct((4,), jnp.int32),
        ),
        in_specs=[smem, smem, pl.BlockSpec(memory_space=pl.ANY)],
        out_specs=(vmem, vmem, vmem, smem),
        scratch_shapes=[
            pltpu.VMEM((2 * SECOND, ROW), jnp.bfloat16),
            pltpu.VMEM((2 * SECOND, ROW), jnp.bfloat16),
            pltpu.SemaphoreType.DMA((2,)),
        ],
        cost_estimate=pl.CostEstimate(flops=100_000, bytes_accessed=400_000, transcendentals=0),
        compiler_params=pltpu.CompilerParams(vmem_limit_bytes=8 << 20),
        name="pick_slots",
    )(pairing, flags, heard)


def far_exchange(slots):
    depth = lax.axis_size("depth")
    groups = [
        [(t + s) * depth + d + e for s in (0, 16) for e in (0, 8)]
        for t in range(16)
        for d in range(8)
    ]
    return lax.all_to_all(slots, ("trainer", "depth"), 0, 0, axis_index_groups=groups)


def exchange_depth(keep, send):
    groups = [list(range(core, 16, 2)) for core in range(2)]
    mine = keep + move(send, "depth", lambda i: i ^ 1).astype(jnp.float32)
    return lax.all_to_all(
        mine.astype(jnp.bfloat16), "depth", 0, 0, axis_index_groups=groups
    )


def shifted(value, by):
    count = lax.axis_size("depth")
    links = [(i, i + by) for i in range(count) if 0 <= i + by < count]
    return lax.ppermute(value, "depth", links)


def critic_forms(disc):
    cube = disc.reshape(2, 2, 2, disc.shape[1], disc.shape[2])
    forward = cube.transpose(3, 0, 2, 1, 4).reshape(ROW, 8 * CH)
    backward = cube.transpose(0, 1, 4, 2, 3).reshape(4 * CH, 2 * ROW)
    return forward, backward


def one_step(noise, gen_weight, gen_momentum, disc_weight, score_weight, pairing, flags):
    together = lax.optimization_barrier
    slab = lax.axis_index("depth").astype(jnp.int32)
    latent = noise[0]
    packed, rows = pack_slots(gen_weight, gen_momentum)
    heard = plane_exchange(packed)
    pieces = (
        shifted(latent[PLANES - 1 :], 2),
        shifted(latent, 1),
        latent,
        shifted(latent, -1),
        shifted(latent[:1], -2),
    )
    critic, critic_back = critic_forms(disc_weight[0])
    score = jnp.broadcast_to(score_weight[0][:, None], (ROW, ROW))
    heard, pieces, critic, critic_back, score = together(
        (heard, pieces, critic, critic_back, score)
    )
    slots, moment_own, moment_other, info = pick_slots(pairing, flags, heard)
    got = far_exchange(slots)
    across = move(moment_other, "trainer", lambda i: i ^ 16)
    held = lax.dynamic_slice_in_dim(got, info[0], 2, 0)
    both = held
    held = jnp.concatenate([held, move(held, "depth", lambda i: i ^ 4)])
    held = jnp.concatenate([held, move(held, "depth", lambda i: i ^ 2)])
    near = move(held, "depth", lambda i: i ^ 1)
    generated, keep, send = local_step(
        slab.reshape(1), pieces, held, near, critic, critic_back, score
    )
    keep, send, across = together((keep, send, across))
    new_weight, new_momentum = update(
        info, rows, both, moment_own, across, exchange_depth(keep, send)
    )
    return generated[None], new_weight, new_momentum


def solution(mesh):
    placed = (
        P("trainer", "depth", None, None),
        P("trainer", "depth"),
        P("trainer", "depth"),
        P("trainer", None, None, None),
        P("trainer", None),
        P(),
        P(),
    )
    return jax.shard_map(
        one_step,
        mesh=mesh,
        in_specs=placed,
        out_specs=(P("trainer", "depth", None, None), P("trainer", "depth"), P("trainer", "depth")),
        check_vma=False,
    )
```

```python
import math

import jax
import jax.numpy as jnp
from jax import lax
from jax.experimental import pallas as pl
from jax.experimental.pallas import tpu as pltpu
from jax.sharding import PartitionSpec as P


CH = 64
ROW = 128
ROWS = 162
SLABS = 16
PLANES = 4
DEPTH = 64
K_ROWS = 27 * CH // 2
FLAT_ROWS = 3 * K_ROWS
momentum_decay = 0.9
step_length = 0.01


def gelu_parts(x):
    c = math.sqrt(2.0 / math.pi)
    square = x * x
    t = jnp.tanh(c * (x + 0.044715 * (x * square)))
    half = 0.5 * (1.0 + t)
    slope = half + 0.5 * x * (1.0 - t * t) * (c * (1.0 + 3.0 * 0.044715 * square))
    return x * half, slope


def local_kernel(
    slab_ref,
    far_low,
    low,
    own,
    high,
    far_high,
    held_ref,
    got_ref,
    critic_ref,
    critic_back_ref,
    score_ref,
    out_ref,
    keep_ref,
    send_ref,
    raw,
    natural,
    forward_w,
    backward_w,
    win0,
    win1,
    win2,
    wing3,
    wing2,
    grad1,
    slope1,
    slope2,
    flat_k,
    flat,
):
    slab = slab_ref[0]
    lane = lax.broadcasted_iota(jnp.int32, (2 * CH, ROW), 1)
    lane_half = lax.broadcasted_iota(jnp.int32, (CH, ROW), 1)

    def store_window(target, index, value):
        target[index, 0:ROW, :] = jnp.where(lane == 0, 0.0, pltpu.roll(value, 1, 1)).astype(
            jnp.bfloat16
        )
        target[index, ROW : 2 * ROW, :] = value.astype(jnp.bfloat16)
        target[index, 2 * ROW : 3 * ROW, :] = jnp.where(
            lane == ROW - 1, 0.0, pltpu.roll(value, ROW - 1, 1)
        ).astype(jnp.bfloat16)

    def inside(plane, value):
        z = slab * PLANES + plane
        return jnp.where(jnp.logical_and(z >= 0, z < DEPTH), value, 0.0)

    sources = (
        [far_low[0]]
        + [low[i] for i in range(PLANES)]
        + [own[i] for i in range(PLANES)]
        + [high[i] for i in range(PLANES)]
        + [far_high[0]]
    )
    for index, plane in enumerate(sources):
        value = jnp.concatenate([plane[:, :ROW], plane[:, ROW:]], axis=0).astype(jnp.float32)
        store_window(win0, index, value)

    for block in range(SLABS):
        apart = block ^ slab
        slot = ((apart >> 1) & 1) * 4 + ((apart >> 2) & 1) * 2 + block // 8
        piece = jnp.where(
            (apart & 1) == 1,
            got_ref[slot].astype(jnp.float32),
            held_ref[slot].astype(jnp.float32),
        )
        raw[block * ROWS : (block + 1) * ROWS, :] = piece

    for layer in range(3):
        rows = raw[layer * K_ROWS : (layer + 1) * K_ROWS, :]
        natural[pl.ds(layer * 2 * K_ROWS, K_ROWS, stride=2), :] = rows
        natural[pl.ds(layer * 2 * K_ROWS + 1, K_ROWS, stride=2), :] = pltpu.roll(rows, CH, 1)

    def kernel_at(layer, a, b, c):
        start = (layer * 27 + 9 * a + 3 * b + c) * CH
        return natural[start : start + CH, :]

    left = lane_half < CH
    for layer in range(3):
        for a in range(3):
            for c in range(3):
                middle = kernel_at(layer, a, 1, c)
                top = jnp.where(left, middle, pltpu.roll(kernel_at(layer, a, 2, c), CH, 1))
                bottom = jnp.where(left, kernel_at(layer, a, 0, c), pltpu.roll(middle, CH, 1))
                block = jnp.concatenate([top, bottom], axis=0)
                spot = (3 * a + c) * ROW
                forward_w[layer, :, spot : spot + ROW] = block.astype(jnp.bfloat16)
                if layer:
                    spot = (3 * (2 - a) + 2 - c) * ROW
                    backward_w[layer - 1, :, spot : spot + ROW] = block.T.astype(jnp.bfloat16)

    def pair_product(weights, windows, index):
        first = windows[index : index + 3].reshape(9 * ROW, ROW)
        second = windows[index + 1 : index + 4].reshape(9 * ROW, ROW)
        return jnp.dot(
            weights,
            jnp.concatenate([first, second], axis=1),
            preferred_element_type=jnp.float32,
        )

    for pair in range(6):
        pre = pair_product(forward_w[0], win0, 2 * pair)
        for side in range(2):
            plane = 2 * pair + side - 4
            value, slope = gelu_parts(pre[:, side * ROW : (side + 1) * ROW])
            if 0 <= plane < PLANES:
                slope1[plane] = slope
            store_window(win1, plane + 4, inside(plane, value))

    for pair in range(5):
        pre = pair_product(forward_w[1], win1, 2 * pair)
        for side in range(2):
            plane = 2 * pair + side - 3
            value, slope = gelu_parts(pre[:, side * ROW : (side + 1) * ROW])
            if -1 <= plane < PLANES + 1:
                slope2[plane + 1] = slope
            store_window(win2, plane + 3, inside(plane, value))

    even = (lane % 2) == 0
    for pair in range(4):
        pre = pair_product(forward_w[2], win2, 2 * pair)
        made = jnp.tanh(pre)
        parts = []
        for side in range(2):
            plane = 2 * pair + side - 2
            shown = made[:, side * ROW : (side + 1) * ROW].astype(jnp.bfloat16)
            if 0 <= plane < PLANES:
                out_ref[plane] = jnp.concatenate([shown[:CH], shown[CH:]], axis=1)
            parts.append(shown)
            parts.append(pltpu.roll(shown.astype(jnp.float32), ROW - 1, 1).astype(jnp.bfloat16))
        response = jnp.dot(
            critic_ref[...], jnp.concatenate(parts, axis=0), preferred_element_type=jnp.float32
        )
        features, slope = gelu_parts(response)
        score = jnp.sum(score_ref[...] * features, axis=0, keepdims=True)
        push = -jax.nn.sigmoid(-score)
        upstream = (slope * (push * score_ref[...])).astype(jnp.bfloat16).astype(jnp.float32)
        upstream = jnp.where(even, upstream, 0.0)
        both = jnp.concatenate(
            [upstream.astype(jnp.bfloat16), pltpu.roll(upstream, 1, 1).astype(jnp.bfloat16)],
            axis=0,
        )
        spread = jnp.dot(critic_back_ref[...], both, preferred_element_type=jnp.float32)
        for side in range(2):
            plane = 2 * pair + side - 2
            t = made[:, side * ROW : (side + 1) * ROW]
            grad = spread[side * ROW : (side + 1) * ROW] * (1.0 - t * t)
            grad = grad.astype(jnp.bfloat16).astype(jnp.float32)
            store_window(wing3, plane + 2, inside(plane, grad))

    def kernel_grad(layer, gradient, windows, offset):
        for a in range(3):
            moved = jnp.concatenate([windows[z + a + offset] for z in range(PLANES)], axis=1)
            product = lax.dot_general(
                gradient, moved, (((1,), (1,)), ((), ())), preferred_element_type=jnp.float32
            )
            for c in range(3):
                block = product[:, c * ROW : (c + 1) * ROW]
                top, bottom = block[:CH], block[CH:]
                values = (bottom, top + pltpu.roll(bottom, CH, 1), pltpu.roll(top, CH, 1))
                for b in range(3):
                    spot = 9 * a + 3 * b + c
                    flat_k[spot * CH : (spot + 1) * CH, :] = values[b]
        evens = flat_k[pl.ds(0, K_ROWS, stride=2), :]
        odds = flat_k[pl.ds(1, K_ROWS, stride=2), :]
        wide = lax.broadcasted_iota(jnp.int32, (K_ROWS, ROW), 1)
        flat[layer * K_ROWS : (layer + 1) * K_ROWS, :] = jnp.where(
            wide < CH, evens, pltpu.roll(odds, CH, 1)
        )

    def centre(windows, offset):
        return jnp.concatenate(
            [windows[z + offset, ROW : 2 * ROW, :] for z in range(PLANES)], axis=1
        )

    kernel_grad(2, centre(wing3, 2), win2, 2)
    for pair in range(3):
        back = pair_product(backward_w[1], wing3, 2 * pair)
        for side in range(2):
            plane = 2 * pair + side - 1
            grad = slope2[plane + 1] * back[:, side * ROW : (side + 1) * ROW]
            grad = grad.astype(jnp.bfloat16).astype(jnp.float32)
            store_window(wing2, plane + 1, inside(plane, grad))
    kernel_grad(1, centre(wing2, 1), win1, 3)
    for pair in range(2):
        back = pair_product(backward_w[0], wing2, 2 * pair)
        for side in range(2):
            plane = 2 * pair + side
            grad = slope1[plane] * back[:, side * ROW : (side + 1) * ROW]
            grad1[:, plane * ROW : (plane + 1) * ROW] = grad.astype(jnp.bfloat16)
    kernel_grad(0, grad1[...], win0, 4)

    for block in range(SLABS):
        apart = block ^ slab
        piece = flat[block * ROWS : (block + 1) * ROWS, :]

        @pl.when((apart & 1) == 1)
        def _():
            send_ref[block // 2] = piece.astype(jnp.bfloat16)

        @pl.when((apart & 1) == 0)
        def _():
            keep_ref[block // 2] = piece


def local_step(slab, pieces, held, got, critic, critic_back, score):
    bf16, f32 = jnp.bfloat16, jnp.float32
    vmem = pl.BlockSpec(memory_space=pltpu.VMEM)
    return pl.pallas_call(
        local_kernel,
        out_shape=(
            jax.ShapeDtypeStruct((PLANES, CH, 2 * ROW), bf16),
            jax.ShapeDtypeStruct((SLABS // 2, ROWS, ROW), f32),
            jax.ShapeDtypeStruct((SLABS // 2, ROWS, ROW), bf16),
        ),
        in_specs=[pl.BlockSpec(memory_space=pltpu.SMEM)] + [vmem] * 10,
        out_specs=(vmem, vmem, vmem),
        scratch_shapes=[
            pltpu.VMEM((FLAT_ROWS, ROW), f32),
            pltpu.VMEM((2 * FLAT_ROWS, ROW), f32),
            pltpu.VMEM((3, ROW, 9 * ROW), bf16),
            pltpu.VMEM((2, ROW, 9 * ROW), bf16),
            pltpu.VMEM((14, 3 * ROW, ROW), bf16),
            pltpu.VMEM((12, 3 * ROW, ROW), bf16),
            pltpu.VMEM((10, 3 * ROW, ROW), bf16),
            pltpu.VMEM((8, 3 * ROW, ROW), bf16),
            pltpu.VMEM((6, 3 * ROW, ROW), bf16),
            pltpu.VMEM((ROW, PLANES * ROW), bf16),
            pltpu.VMEM((PLANES, ROW, ROW), f32),
            pltpu.VMEM((PLANES + 2, ROW, ROW), f32),
            pltpu.VMEM((2 * K_ROWS, ROW), f32),
            pltpu.VMEM((FLAT_ROWS, ROW), f32),
        ],
        compiler_params=pltpu.CompilerParams(vmem_limit_bytes=24 << 20),
        cost_estimate=pl.CostEstimate(
            flops=6_000_000_000, bytes_accessed=4_000_000, transcendentals=1_000_000
        ),
        name="local_step",
    )(slab, *pieces, held, got, critic, critic_back, score)


def move(value, axis, target_of):
    count = lax.axis_size(axis)
    return lax.ppermute(value, axis, [(i, target_of(i)) for i in range(count)])


def plane_exchange(slots):
    groups = [list(range(16)), list(range(16, 32))]
    return lax.all_to_all(slots, "trainer", 0, 0, axis_index_groups=groups)


def pack_kernel(weight_ref, moment_ref, out_ref, own_ref, rows_ref):
    for index, source in enumerate((weight_ref, moment_ref)):
        for r in range(ROWS):
            rows_ref[index, r : r + 1, :] = source[:, r * ROW : (r + 1) * ROW]
    packed = rows_ref[0].astype(jnp.bfloat16)
    for slot in range(16):
        out_ref[slot] = packed
    own_ref[...] = rows_ref[1].astype(jnp.bfloat16)


def pack_slots(weight, moment):
    vmem = pl.BlockSpec(memory_space=pltpu.VMEM)
    return pl.pallas_call(
        pack_kernel,
        out_shape=(
            jax.ShapeDtypeStruct((16, ROWS, ROW), jnp.bfloat16),
            jax.ShapeDtypeStruct((ROWS, ROW), jnp.bfloat16),
            jax.ShapeDtypeStruct((2, ROWS, ROW), jnp.float32),
        ),
        in_specs=[vmem, vmem],
        out_specs=(vmem, vmem, vmem),
        cost_estimate=pl.CostEstimate(flops=100_000, bytes_accessed=1_000_000, transcendentals=0),
        name="pack_slots",
    )(weight, moment)


def pick_kernel(pairing, flags, heard, slots, info, for_own, for_other, sems):
    rank = lax.axis_index("trainer")
    half = rank >> 4
    across = rank ^ 16
    source = jnp.where(flags[rank] == 1, rank, pairing[rank])
    other = jnp.where(flags[across] == 1, across, pairing[across])
    first = pltpu.make_async_copy(heard.at[source & 15], for_own, sems.at[0])
    second = pltpu.make_async_copy(heard.at[other & 15], for_other, sems.at[1])
    first.start()
    second.start()
    info[0] = 2 * (source >> 4)
    info[1] = pairing[rank] & 15
    info[2] = flags[rank]
    info[3] = half
    first.wait()
    second.wait()
    for member in range(4):
        slots[member] = jnp.where(half == member // 2, for_own[...], for_other[...])


def pick_slots(pairing, flags, heard):
    vmem = pl.BlockSpec(memory_space=pltpu.VMEM)
    smem = pl.BlockSpec(memory_space=pltpu.SMEM)
    return pl.pallas_call(
        pick_kernel,
        out_shape=(
            jax.ShapeDtypeStruct((4, ROWS, ROW), jnp.bfloat16),
            jax.ShapeDtypeStruct((4,), jnp.int32),
        ),
        in_specs=[smem, smem, pl.BlockSpec(memory_space=pl.ANY)],
        out_specs=(vmem, smem),
        scratch_shapes=[
            pltpu.VMEM((ROWS, ROW), jnp.bfloat16),
            pltpu.VMEM((ROWS, ROW), jnp.bfloat16),
            pltpu.SemaphoreType.DMA((2,)),
        ],
        cost_estimate=pl.CostEstimate(flops=100_000, bytes_accessed=300_000, transcendentals=0),
        compiler_params=pltpu.CompilerParams(vmem_limit_bytes=8 << 20),
        name="pick_slots",
    )(pairing, flags, heard)


def moment_kernel(pairing, own, across, out_ref):
    half = lax.axis_index("trainer") >> 4
    for slot in range(16):
        here = (pairing[half * 16 + slot] >> 4) == half
        out_ref[slot] = jnp.where(here, own[...], across[...])


def moment_slots(pairing, own, across):
    vmem = pl.BlockSpec(memory_space=pltpu.VMEM)
    return pl.pallas_call(
        moment_kernel,
        out_shape=jax.ShapeDtypeStruct((16, ROWS, ROW), jnp.bfloat16),
        in_specs=[pl.BlockSpec(memory_space=pltpu.SMEM), vmem, vmem],
        out_specs=vmem,
        cost_estimate=pl.CostEstimate(flops=100_000, bytes_accessed=800_000, transcendentals=0),
        compiler_params=pltpu.CompilerParams(vmem_limit_bytes=8 << 20),
        name="moment_slots",
    )(pairing, own, across)


def update_kernel(info, rows, held, moments, heard, weight_ref, moment_ref, other, fresh, sem):
    fetch = pltpu.make_async_copy(moments.at[info[1]], other, sem)
    fetch.start()
    grad = heard[0].astype(jnp.float32)
    for member in range(1, heard.shape[0]):
        grad = grad + heard[member].astype(jnp.float32)
    keeper = info[2] == 1
    far = lax.axis_index("depth") >> 3
    weight = jnp.where(keeper, rows[0], held[far].astype(jnp.float32))
    fetch.wait()
    moment = jnp.where(keeper, rows[1], other[...].astype(jnp.float32))
    moment = momentum_decay * moment + grad
    fresh[0] = weight - step_length * moment
    fresh[1] = moment
    for index, target in enumerate((weight_ref, moment_ref)):
        for r in range(ROWS):
            target[:, r * ROW : (r + 1) * ROW] = fresh[index, r : r + 1, :]


def update(info, rows, held, moments, heard):
    vmem = pl.BlockSpec(memory_space=pltpu.VMEM)
    flat = jax.ShapeDtypeStruct((1, ROWS * ROW), jnp.float32)
    return pl.pallas_call(
        update_kernel,
        out_shape=(flat, flat),
        in_specs=[
            pl.BlockSpec(memory_space=pltpu.SMEM),
            vmem,
            vmem,
            pl.BlockSpec(memory_space=pl.ANY),
            vmem,
        ],
        out_specs=(vmem, vmem),
        scratch_shapes=[
            pltpu.VMEM((ROWS, ROW), jnp.bfloat16),
            pltpu.VMEM((2, ROWS, ROW), jnp.float32),
            pltpu.SemaphoreType.DMA,
        ],
        cost_estimate=pl.CostEstimate(flops=500_000, bytes_accessed=1_000_000, transcendentals=0),
        compiler_params=pltpu.CompilerParams(vmem_limit_bytes=8 << 20),
        name="update",
    )(info, rows, held, moments, heard)


def far_exchange(slots):
    depth = lax.axis_size("depth")
    groups = [
        [(t + s) * depth + d + e for s in (0, 16) for e in (0, 8)]
        for t in range(16)
        for d in range(8)
    ]
    return lax.all_to_all(slots, ("trainer", "depth"), 0, 0, axis_index_groups=groups)


def exchange_depth(keep, send):
    groups = [list(range(core, 16, 2)) for core in range(2)]
    mine = keep + move(send, "depth", lambda i: i ^ 1).astype(jnp.float32)
    return lax.all_to_all(
        mine.astype(jnp.bfloat16), "depth", 0, 0, axis_index_groups=groups
    )


def shifted(value, by):
    count = lax.axis_size("depth")
    links = [(i, i + by) for i in range(count) if 0 <= i + by < count]
    return lax.ppermute(value, "depth", links)


def critic_forms(disc):
    cube = disc.reshape(2, 2, 2, disc.shape[1], disc.shape[2])
    forward = cube.transpose(3, 0, 2, 1, 4).reshape(ROW, 8 * CH)
    backward = cube.transpose(0, 1, 4, 2, 3).reshape(4 * CH, 2 * ROW)
    return forward, backward


def one_step(noise, gen_weight, gen_momentum, disc_weight, score_weight, pairing, flags):
    together = lax.optimization_barrier
    slab = lax.axis_index("depth").astype(jnp.int32)
    latent = noise[0]
    packed, own_moment, rows = pack_slots(gen_weight, gen_momentum)
    heard = plane_exchange(packed)
    low, high = shifted(latent, 1), shifted(latent, -1)
    critic, critic_back = critic_forms(disc_weight[0])
    score = jnp.broadcast_to(score_weight[0][:, None], (ROW, ROW))
    heard, low, high, critic, critic_back, score = together(
        (heard, low, high, critic, critic_back, score)
    )
    slots, info = pick_slots(pairing, flags, heard)
    got = far_exchange(slots)
    across = move(own_moment, "trainer", lambda i: i ^ 16)
    held = lax.dynamic_slice_in_dim(got, info[0], 2, 0)
    both = held
    held = jnp.concatenate([held, move(held, "depth", lambda i: i ^ 4)])
    far_low = shifted(latent[PLANES - 1 :], 2)
    far_high = shifted(latent[:1], -2)
    moments = moment_slots(pairing, own_moment, across)
    held, far_low, far_high, moments = together((held, far_low, far_high, moments))
    held = jnp.concatenate([held, move(held, "depth", lambda i: i ^ 2)])
    moments = plane_exchange(moments)
    near = move(held, "depth", lambda i: i ^ 1)
    pieces = (far_low, low, latent, high, far_high)
    generated, keep, send = local_step(
        slab.reshape(1), pieces, held, near, critic, critic_back, score
    )
    keep, send, moments = together((keep, send, moments))
    sums = exchange_depth(keep, send)
    new_weight, new_momentum = update(info, rows, both, moments, sums)
    return generated[None], new_weight, new_momentum


def solution(mesh):
    placed = (
        P("trainer", "depth", None, None),
        P("trainer", "depth"),
        P("trainer", "depth"),
        P("trainer", None, None, None),
        P("trainer", None),
        P(),
        P(),
    )
    return jax.shard_map(
        one_step,
        mesh=mesh,
        in_specs=placed,
        out_specs=(P("trainer", "depth", None, None), P("trainer", "depth"), P("trainer", "depth")),
        check_vma=False,
    )
```

```python
import math

import jax
import jax.numpy as jnp
from jax import lax
from jax.experimental import pallas as pl
from jax.experimental.pallas import tpu as pltpu
from jax.sharding import PartitionSpec as P


CH = 64
ROW = 128
ROWS = 162
SECOND = 168
SLABS = 16
PLANES = 4
DEPTH = 64
K_ROWS = 27 * CH // 2
FLAT_ROWS = 3 * K_ROWS
momentum_decay = 0.9
step_length = 0.01


def gelu_parts(x):
    c = math.sqrt(2.0 / math.pi)
    square = x * x
    t = jnp.tanh(c * (x + 0.044715 * (x * square)))
    half = 0.5 * (1.0 + t)
    slope = half + 0.5 * x * (1.0 - t * t) * (c * (1.0 + 3.0 * 0.044715 * square))
    return x * half, slope


def local_kernel(
    slab_ref,
    far_low,
    low,
    own,
    high,
    far_high,
    held_ref,
    critic_ref,
    critic_back_ref,
    score_ref,
    out_ref,
    keep_ref,
    send_ref,
    raw,
    natural,
    forward_w,
    backward_w,
    win0,
    win1,
    win2,
    wing3,
    wing2,
    grad1,
    slope1,
    slope2,
    flat_k,
    flat,
):
    slab = slab_ref[0]
    lane = lax.broadcasted_iota(jnp.int32, (2 * CH, ROW), 1)
    lane_half = lax.broadcasted_iota(jnp.int32, (CH, ROW), 1)

    def store_window(target, index, value):
        target[index, 0:ROW, :] = jnp.where(lane == 0, 0.0, pltpu.roll(value, 1, 1)).astype(
            jnp.bfloat16
        )
        target[index, ROW : 2 * ROW, :] = value.astype(jnp.bfloat16)
        target[index, 2 * ROW : 3 * ROW, :] = jnp.where(
            lane == ROW - 1, 0.0, pltpu.roll(value, ROW - 1, 1)
        ).astype(jnp.bfloat16)

    def inside(plane, value):
        z = slab * PLANES + plane
        return jnp.where(jnp.logical_and(z >= 0, z < DEPTH), value, 0.0)

    sources = (
        [far_low[0]]
        + [low[i] for i in range(PLANES)]
        + [own[i] for i in range(PLANES)]
        + [high[i] for i in range(PLANES)]
        + [far_high[0]]
    )
    for index, plane in enumerate(sources):
        value = jnp.concatenate([plane[:, :ROW], plane[:, ROW:]], axis=0).astype(jnp.float32)
        store_window(win0, index, value)

    for block in range(SLABS):
        slot = ((block >> 2) ^ (slab >> 2)) % 2 * 2 + block // 8
        raw[block * ROWS : (block + 1) * ROWS, :] = held_ref[block % 4, slot].astype(jnp.float32)

    for layer in range(3):
        rows = raw[layer * K_ROWS : (layer + 1) * K_ROWS, :]
        natural[pl.ds(layer * 2 * K_ROWS, K_ROWS, stride=2), :] = rows
        natural[pl.ds(layer * 2 * K_ROWS + 1, K_ROWS, stride=2), :] = pltpu.roll(rows, CH, 1)

    def kernel_at(layer, a, b, c):
        start = (layer * 27 + 9 * a + 3 * b + c) * CH
        return natural[start : start + CH, :]

    left = lane_half < CH
    for layer in range(3):
        for a in range(3):
            for c in range(3):
                middle = kernel_at(layer, a, 1, c)
                top = jnp.where(left, middle, pltpu.roll(kernel_at(layer, a, 2, c), CH, 1))
                bottom = jnp.where(left, kernel_at(layer, a, 0, c), pltpu.roll(middle, CH, 1))
                block = jnp.concatenate([top, bottom], axis=0)
                spot = (3 * a + c) * ROW
                forward_w[layer, :, spot : spot + ROW] = block.astype(jnp.bfloat16)
                if layer:
                    spot = (3 * (2 - a) + 2 - c) * ROW
                    backward_w[layer - 1, :, spot : spot + ROW] = block.T.astype(jnp.bfloat16)

    def pair_product(weights, windows, index):
        first = windows[index : index + 3].reshape(9 * ROW, ROW)
        second = windows[index + 1 : index + 4].reshape(9 * ROW, ROW)
        return jnp.dot(
            weights,
            jnp.concatenate([first, second], axis=1),
            preferred_element_type=jnp.float32,
        )

    for pair in range(6):
        pre = pair_product(forward_w[0], win0, 2 * pair)
        for side in range(2):
            plane = 2 * pair + side - 4
            value, slope = gelu_parts(pre[:, side * ROW : (side + 1) * ROW])
            if 0 <= plane < PLANES:
                slope1[plane] = slope
            store_window(win1, plane + 4, inside(plane, value))

    for pair in range(5):
        pre = pair_product(forward_w[1], win1, 2 * pair)
        for side in range(2):
            plane = 2 * pair + side - 3
            value, slope = gelu_parts(pre[:, side * ROW : (side + 1) * ROW])
            if -1 <= plane < PLANES + 1:
                slope2[plane + 1] = slope
            store_window(win2, plane + 3, inside(plane, value))

    even = (lane % 2) == 0
    for pair in range(4):
        pre = pair_product(forward_w[2], win2, 2 * pair)
        made = jnp.tanh(pre)
        parts = []
        for side in range(2):
            plane = 2 * pair + side - 2
            shown = made[:, side * ROW : (side + 1) * ROW].astype(jnp.bfloat16)
            if 0 <= plane < PLANES:
                out_ref[plane] = jnp.concatenate([shown[:CH], shown[CH:]], axis=1)
            parts.append(shown)
            parts.append(pltpu.roll(shown.astype(jnp.float32), ROW - 1, 1).astype(jnp.bfloat16))
        response = jnp.dot(
            critic_ref[...], jnp.concatenate(parts, axis=0), preferred_element_type=jnp.float32
        )
        features, slope = gelu_parts(response)
        score = jnp.sum(score_ref[...] * features, axis=0, keepdims=True)
        push = -jax.nn.sigmoid(-score)
        upstream = (slope * (push * score_ref[...])).astype(jnp.bfloat16).astype(jnp.float32)
        upstream = jnp.where(even, upstream, 0.0)
        both = jnp.concatenate(
            [upstream.astype(jnp.bfloat16), pltpu.roll(upstream, 1, 1).astype(jnp.bfloat16)],
            axis=0,
        )
        spread = jnp.dot(critic_back_ref[...], both, preferred_element_type=jnp.float32)
        for side in range(2):
            plane = 2 * pair + side - 2
            t = made[:, side * ROW : (side + 1) * ROW]
            grad = spread[side * ROW : (side + 1) * ROW] * (1.0 - t * t)
            grad = grad.astype(jnp.bfloat16).astype(jnp.float32)
            store_window(wing3, plane + 2, inside(plane, grad))

    def kernel_grad(layer, gradient, windows, offset):
        for a in range(3):
            moved = jnp.concatenate([windows[z + a + offset] for z in range(PLANES)], axis=1)
            product = lax.dot_general(
                gradient, moved, (((1,), (1,)), ((), ())), preferred_element_type=jnp.float32
            )
            for c in range(3):
                block = product[:, c * ROW : (c + 1) * ROW]
                top, bottom = block[:CH], block[CH:]
                values = (bottom, top + pltpu.roll(bottom, CH, 1), pltpu.roll(top, CH, 1))
                for b in range(3):
                    spot = 9 * a + 3 * b + c
                    flat_k[spot * CH : (spot + 1) * CH, :] = values[b]
        evens = flat_k[pl.ds(0, K_ROWS, stride=2), :]
        odds = flat_k[pl.ds(1, K_ROWS, stride=2), :]
        wide = lax.broadcasted_iota(jnp.int32, (K_ROWS, ROW), 1)
        flat[layer * K_ROWS : (layer + 1) * K_ROWS, :] = jnp.where(
            wide < CH, evens, pltpu.roll(odds, CH, 1)
        )

    def centre(windows, offset):
        return jnp.concatenate(
            [windows[z + offset, ROW : 2 * ROW, :] for z in range(PLANES)], axis=1
        )

    kernel_grad(2, centre(wing3, 2), win2, 2)
    for pair in range(3):
        back = pair_product(backward_w[1], wing3, 2 * pair)
        for side in range(2):
            plane = 2 * pair + side - 1
            grad = slope2[plane + 1] * back[:, side * ROW : (side + 1) * ROW]
            grad = grad.astype(jnp.bfloat16).astype(jnp.float32)
            store_window(wing2, plane + 1, inside(plane, grad))
    kernel_grad(1, centre(wing2, 1), win1, 3)
    for pair in range(2):
        back = pair_product(backward_w[0], wing2, 2 * pair)
        for side in range(2):
            plane = 2 * pair + side
            grad = slope1[plane] * back[:, side * ROW : (side + 1) * ROW]
            grad1[:, plane * ROW : (plane + 1) * ROW] = grad.astype(jnp.bfloat16)
    kernel_grad(0, grad1[...], win0, 4)

    for block in range(SLABS):
        apart = block ^ slab
        piece = flat[block * ROWS : (block + 1) * ROWS, :]

        @pl.when((apart & 1) == 1)
        def _():
            send_ref[block // 2] = piece.astype(jnp.bfloat16)

        @pl.when((apart & 1) == 0)
        def _():
            keep_ref[block // 2] = piece


def local_step(slab, pieces, held, critic, critic_back, score):
    bf16, f32 = jnp.bfloat16, jnp.float32
    vmem = pl.BlockSpec(memory_space=pltpu.VMEM)
    return pl.pallas_call(
        local_kernel,
        out_shape=(
            jax.ShapeDtypeStruct((PLANES, CH, 2 * ROW), bf16),
            jax.ShapeDtypeStruct((SLABS // 2, ROWS, ROW), f32),
            jax.ShapeDtypeStruct((SLABS // 2, ROWS, ROW), bf16),
        ),
        in_specs=[pl.BlockSpec(memory_space=pltpu.SMEM)] + [vmem] * 9,
        out_specs=(vmem, vmem, vmem),
        scratch_shapes=[
            pltpu.VMEM((FLAT_ROWS, ROW), f32),
            pltpu.VMEM((2 * FLAT_ROWS, ROW), f32),
            pltpu.VMEM((3, ROW, 9 * ROW), bf16),
            pltpu.VMEM((2, ROW, 9 * ROW), bf16),
            pltpu.VMEM((14, 3 * ROW, ROW), bf16),
            pltpu.VMEM((12, 3 * ROW, ROW), bf16),
            pltpu.VMEM((10, 3 * ROW, ROW), bf16),
            pltpu.VMEM((8, 3 * ROW, ROW), bf16),
            pltpu.VMEM((6, 3 * ROW, ROW), bf16),
            pltpu.VMEM((ROW, PLANES * ROW), bf16),
            pltpu.VMEM((PLANES, ROW, ROW), f32),
            pltpu.VMEM((PLANES + 2, ROW, ROW), f32),
            pltpu.VMEM((2 * K_ROWS, ROW), f32),
            pltpu.VMEM((FLAT_ROWS, ROW), f32),
        ],
        compiler_params=pltpu.CompilerParams(vmem_limit_bytes=24 << 20),
        cost_estimate=pl.CostEstimate(
            flops=6_000_000_000, bytes_accessed=4_000_000, transcendentals=1_000_000
        ),
        name="local_step",
    )(slab, *pieces, held, critic, critic_back, score)


def move(value, axis, target_of):
    count = lax.axis_size(axis)
    return lax.ppermute(value, axis, [(i, target_of(i)) for i in range(count)])


def plane_exchange(slots):
    groups = [list(range(16)), list(range(16, 32))]
    return lax.all_to_all(slots, "trainer", 0, 0, axis_index_groups=groups)


def pack_kernel(weight_ref, moment_ref, out_ref, rows):
    rows[...] = jnp.zeros(rows.shape, jnp.float32)
    for index, source in enumerate((weight_ref, moment_ref)):
        for r in range(ROWS):
            spot = index * SECOND + r
            rows[spot : spot + 1, :] = source[:, r * ROW : (r + 1) * ROW]
    packed = rows[...].astype(jnp.bfloat16)
    for slot in range(16):
        out_ref[slot] = packed


def pack_slots(weight, moment):
    vmem = pl.BlockSpec(memory_space=pltpu.VMEM)
    return pl.pallas_call(
        pack_kernel,
        out_shape=(
            jax.ShapeDtypeStruct((16, 2 * SECOND, ROW), jnp.bfloat16),
            jax.ShapeDtypeStruct((2 * SECOND, ROW), jnp.float32),
        ),
        in_specs=[vmem, vmem],
        out_specs=(vmem, vmem),
        cost_estimate=pl.CostEstimate(flops=100_000, bytes_accessed=1_500_000, transcendentals=0),
        name="pack_slots",
    )(weight, moment)


def update_kernel(info, rows, held, moment_own, across, heard, weight_ref, moment_ref, fresh):
    grad = heard[0].astype(jnp.float32)
    for member in range(1, heard.shape[0]):
        grad = grad + heard[member].astype(jnp.float32)
    keeper = info[2] == 1
    far = lax.axis_index("depth") >> 3
    other_weight = held[far].astype(jnp.float32)
    other_moment = jnp.where(
        info[1] == 1, moment_own[...].astype(jnp.float32), across[...].astype(jnp.float32)
    )
    weight = jnp.where(keeper, rows[0:ROWS, :], other_weight)
    moment = jnp.where(keeper, rows[SECOND : SECOND + ROWS, :], other_moment)
    moment = momentum_decay * moment + grad
    fresh[0] = weight - step_length * moment
    fresh[1] = moment
    for index, target in enumerate((weight_ref, moment_ref)):
        for r in range(ROWS):
            target[:, r * ROW : (r + 1) * ROW] = fresh[index, r : r + 1, :]


def update(info, rows, held, moment_own, across, heard):
    vmem = pl.BlockSpec(memory_space=pltpu.VMEM)
    flat = jax.ShapeDtypeStruct((1, ROWS * ROW), jnp.float32)
    return pl.pallas_call(
        update_kernel,
        out_shape=(flat, flat),
        in_specs=[pl.BlockSpec(memory_space=pltpu.SMEM)] + [vmem] * 5,
        out_specs=(vmem, vmem),
        scratch_shapes=[pltpu.VMEM((2, ROWS, ROW), jnp.float32)],
        cost_estimate=pl.CostEstimate(flops=500_000, bytes_accessed=1_000_000, transcendentals=0),
        compiler_params=pltpu.CompilerParams(vmem_limit_bytes=8 << 20),
        name="update",
    )(info, rows, held, moment_own, across, heard)


def pick_kernel(
    pairing, flags, heard, slots, moment_own, moment_other, info, for_own, for_other, sems
):
    rank = lax.axis_index("trainer")
    half = rank >> 4
    across = rank ^ 16
    source = jnp.where(flags[rank] == 1, rank, pairing[rank])
    other = jnp.where(flags[across] == 1, across, pairing[across])
    first = pltpu.make_async_copy(heard.at[source & 15], for_own, sems.at[0])
    second = pltpu.make_async_copy(heard.at[other & 15], for_other, sems.at[1])
    first.start()
    second.start()
    info[0] = 2 * (source >> 4)
    info[1] = jnp.where((source >> 4) == half, 1, 0)
    info[2] = flags[rank]
    info[3] = half
    first.wait()
    second.wait()
    for member in range(4):
        slots[member] = jnp.where(half == member // 2, for_own[0:ROWS, :], for_other[0:ROWS, :])
    moment_own[...] = for_own[SECOND : SECOND + ROWS, :]
    moment_other[...] = for_other[SECOND : SECOND + ROWS, :]


def pick_slots(pairing, flags, heard):
    vmem = pl.BlockSpec(memory_space=pltpu.VMEM)
    smem = pl.BlockSpec(memory_space=pltpu.SMEM)
    share = jax.ShapeDtypeStruct((ROWS, ROW), jnp.bfloat16)
    return pl.pallas_call(
        pick_kernel,
        out_shape=(
            jax.ShapeDtypeStruct((4, ROWS, ROW), jnp.bfloat16),
            share,
            share,
            jax.ShapeDtypeStruct((4,), jnp.int32),
        ),
        in_specs=[smem, smem, pl.BlockSpec(memory_space=pl.ANY)],
        out_specs=(vmem, vmem, vmem, smem),
        scratch_shapes=[
            pltpu.VMEM((2 * SECOND, ROW), jnp.bfloat16),
            pltpu.VMEM((2 * SECOND, ROW), jnp.bfloat16),
            pltpu.SemaphoreType.DMA((2,)),
        ],
        cost_estimate=pl.CostEstimate(flops=100_000, bytes_accessed=400_000, transcendentals=0),
        compiler_params=pltpu.CompilerParams(vmem_limit_bytes=8 << 20),
        name="pick_slots",
    )(pairing, flags, heard)


def far_exchange(slots):
    depth = lax.axis_size("depth")
    groups = [
        [(t + s) * depth + d + e for s in (0, 16) for e in (0, 8)]
        for t in range(16)
        for d in range(8)
    ]
    return lax.all_to_all(slots, ("trainer", "depth"), 0, 0, axis_index_groups=groups)


def exchange_depth(keep, send):
    groups = [list(range(core, 16, 2)) for core in range(2)]
    mine = keep + move(send, "depth", lambda i: i ^ 1).astype(jnp.float32)
    return lax.all_to_all(
        mine.astype(jnp.bfloat16), "depth", 0, 0, axis_index_groups=groups
    )


def shifted(value, by):
    count = lax.axis_size("depth")
    links = [(i, i + by) for i in range(count) if 0 <= i + by < count]
    return lax.ppermute(value, "depth", links)


def critic_forms(disc):
    cube = disc.reshape(2, 2, 2, disc.shape[1], disc.shape[2])
    forward = cube.transpose(3, 0, 2, 1, 4).reshape(ROW, 8 * CH)
    backward = cube.transpose(0, 1, 4, 2, 3).reshape(4 * CH, 2 * ROW)
    return forward, backward


def one_step(noise, gen_weight, gen_momentum, disc_weight, score_weight, pairing, flags):
    together = lax.optimization_barrier
    slab = lax.axis_index("depth").astype(jnp.int32)
    latent = noise[0]
    packed, rows = pack_slots(gen_weight, gen_momentum)
    heard = plane_exchange(packed)
    pieces = (
        shifted(latent[PLANES - 1 :], 2),
        shifted(latent, 1),
        latent,
        shifted(latent, -1),
        shifted(latent[:1], -2),
    )
    critic, critic_back = critic_forms(disc_weight[0])
    score = jnp.broadcast_to(score_weight[0][:, None], (ROW, ROW))
    heard, pieces, critic, critic_back, score = together(
        (heard, pieces, critic, critic_back, score)
    )
    slots, moment_own, moment_other, info = pick_slots(pairing, flags, heard)
    got = far_exchange(slots)
    across = move(moment_other, "trainer", lambda i: i ^ 16)
    held = lax.dynamic_slice_in_dim(got, info[0], 2, 0)
    both = held
    held = jnp.concatenate([held, move(held, "depth", lambda i: i ^ 4)])
    near = [list(range(first, first + 4)) for first in range(0, 16, 4)]
    held = lax.all_gather(held, "depth", axis_index_groups=near)
    generated, keep, send = local_step(
        slab.reshape(1), pieces, held, critic, critic_back, score
    )
    keep, send, across = together((keep, send, across))
    new_weight, new_momentum = update(
        info, rows, both, moment_own, across, exchange_depth(keep, send)
    )
    return generated[None], new_weight, new_momentum


def solution(mesh):
    placed = (
        P("trainer", "depth", None, None),
        P("trainer", "depth"),
        P("trainer", "depth"),
        P("trainer", None, None, None),
        P("trainer", None),
        P(),
        P(),
    )
    return jax.shard_map(
        one_step,
        mesh=mesh,
        in_specs=placed,
        out_specs=(P("trainer", "depth", None, None), P("trainer", "depth"), P("trainer", "depth")),
        check_vma=False,
    )
```

```python
import math

import jax
import jax.numpy as jnp
from jax import lax
from jax.experimental import pallas as pl
from jax.experimental.pallas import tpu as pltpu
from jax.sharding import PartitionSpec as P


CH = 64
ROW = 128
ROWS = 162
SECOND = 168
SLABS = 16
PLANES = 4
DEPTH = 64
K_ROWS = 27 * CH // 2
FLAT_ROWS = 3 * K_ROWS
momentum_decay = 0.9
step_length = 0.01


def gelu_parts(x):
    c = math.sqrt(2.0 / math.pi)
    square = x * x
    t = jnp.tanh(c * (x + 0.044715 * (x * square)))
    half = 0.5 * (1.0 + t)
    slope = half + 0.5 * x * (1.0 - t * t) * (c * (1.0 + 3.0 * 0.044715 * square))
    return x * half, slope


def local_kernel(
    slab_ref,
    far_low,
    low,
    own,
    high,
    far_high,
    held_ref,
    critic_ref,
    critic_back_ref,
    score_ref,
    out_ref,
    keep_ref,
    send_ref,
    raw,
    natural,
    forward_w,
    backward_w,
    win0,
    win1,
    win2,
    wing3,
    wing2,
    grad1,
    slope1,
    slope2,
    flat_k,
    flat,
):
    slab = slab_ref[0]
    lane = lax.broadcasted_iota(jnp.int32, (2 * CH, ROW), 1)
    lane_half = lax.broadcasted_iota(jnp.int32, (CH, ROW), 1)

    def store_window(target, index, value):
        target[index, 0:ROW, :] = jnp.where(lane == 0, 0.0, pltpu.roll(value, 1, 1)).astype(
            jnp.bfloat16
        )
        target[index, ROW : 2 * ROW, :] = value.astype(jnp.bfloat16)
        target[index, 2 * ROW : 3 * ROW, :] = jnp.where(
            lane == ROW - 1, 0.0, pltpu.roll(value, ROW - 1, 1)
        ).astype(jnp.bfloat16)

    def inside(plane, value):
        z = slab * PLANES + plane
        return jnp.where(jnp.logical_and(z >= 0, z < DEPTH), value, 0.0)

    sources = (
        [far_low[0]]
        + [low[i] for i in range(PLANES)]
        + [own[i] for i in range(PLANES)]
        + [high[i] for i in range(PLANES)]
        + [far_high[0]]
    )
    for index, plane in enumerate(sources):
        value = jnp.concatenate([plane[:, :ROW], plane[:, ROW:]], axis=0).astype(jnp.float32)
        store_window(win0, index, value)

    for block in range(SLABS):
        piece = held_ref[block % 8, block // 8]
        raw[block * ROWS : (block + 1) * ROWS, :] = piece.astype(jnp.float32)

    for layer in range(3):
        rows = raw[layer * K_ROWS : (layer + 1) * K_ROWS, :]
        natural[pl.ds(layer * 2 * K_ROWS, K_ROWS, stride=2), :] = rows
        natural[pl.ds(layer * 2 * K_ROWS + 1, K_ROWS, stride=2), :] = pltpu.roll(rows, CH, 1)

    def kernel_at(layer, a, b, c):
        start = (layer * 27 + 9 * a + 3 * b + c) * CH
        return natural[start : start + CH, :]

    left = lane_half < CH
    for layer in range(3):
        for a in range(3):
            for c in range(3):
                middle = kernel_at(layer, a, 1, c)
                top = jnp.where(left, middle, pltpu.roll(kernel_at(layer, a, 2, c), CH, 1))
                bottom = jnp.where(left, kernel_at(layer, a, 0, c), pltpu.roll(middle, CH, 1))
                block = jnp.concatenate([top, bottom], axis=0)
                spot = (3 * a + c) * ROW
                forward_w[layer, :, spot : spot + ROW] = block.astype(jnp.bfloat16)
                if layer:
                    spot = (3 * (2 - a) + 2 - c) * ROW
                    backward_w[layer - 1, :, spot : spot + ROW] = block.T.astype(jnp.bfloat16)

    def pair_product(weights, windows, index):
        first = windows[index : index + 3].reshape(9 * ROW, ROW)
        second = windows[index + 1 : index + 4].reshape(9 * ROW, ROW)
        return jnp.dot(
            weights,
            jnp.concatenate([first, second], axis=1),
            preferred_element_type=jnp.float32,
        )

    for pair in range(6):
        pre = pair_product(forward_w[0], win0, 2 * pair)
        for side in range(2):
            plane = 2 * pair + side - 4
            value, slope = gelu_parts(pre[:, side * ROW : (side + 1) * ROW])
            if 0 <= plane < PLANES:
                slope1[plane] = slope
            store_window(win1, plane + 4, inside(plane, value))

    for pair in range(5):
        pre = pair_product(forward_w[1], win1, 2 * pair)
        for side in range(2):
            plane = 2 * pair + side - 3
            value, slope = gelu_parts(pre[:, side * ROW : (side + 1) * ROW])
            if -1 <= plane < PLANES + 1:
                slope2[plane + 1] = slope
            store_window(win2, plane + 3, inside(plane, value))

    even = (lane % 2) == 0
    for pair in range(4):
        pre = pair_product(forward_w[2], win2, 2 * pair)
        made = jnp.tanh(pre)
        parts = []
        for side in range(2):
            plane = 2 * pair + side - 2
            shown = made[:, side * ROW : (side + 1) * ROW].astype(jnp.bfloat16)
            if 0 <= plane < PLANES:
                out_ref[plane] = jnp.concatenate([shown[:CH], shown[CH:]], axis=1)
            parts.append(shown)
            parts.append(pltpu.roll(shown.astype(jnp.float32), ROW - 1, 1).astype(jnp.bfloat16))
        response = jnp.dot(
            critic_ref[...], jnp.concatenate(parts, axis=0), preferred_element_type=jnp.float32
        )
        features, slope = gelu_parts(response)
        score = jnp.sum(score_ref[...] * features, axis=0, keepdims=True)
        push = -jax.nn.sigmoid(-score)
        upstream = (slope * (push * score_ref[...])).astype(jnp.bfloat16).astype(jnp.float32)
        upstream = jnp.where(even, upstream, 0.0)
        both = jnp.concatenate(
            [upstream.astype(jnp.bfloat16), pltpu.roll(upstream, 1, 1).astype(jnp.bfloat16)],
            axis=0,
        )
        spread = jnp.dot(critic_back_ref[...], both, preferred_element_type=jnp.float32)
        for side in range(2):
            plane = 2 * pair + side - 2
            t = made[:, side * ROW : (side + 1) * ROW]
            grad = spread[side * ROW : (side + 1) * ROW] * (1.0 - t * t)
            grad = grad.astype(jnp.bfloat16).astype(jnp.float32)
            store_window(wing3, plane + 2, inside(plane, grad))

    def kernel_grad(layer, gradient, windows, offset):
        for a in range(3):
            moved = jnp.concatenate([windows[z + a + offset] for z in range(PLANES)], axis=1)
            product = lax.dot_general(
                gradient, moved, (((1,), (1,)), ((), ())), preferred_element_type=jnp.float32
            )
            for c in range(3):
                block = product[:, c * ROW : (c + 1) * ROW]
                top, bottom = block[:CH], block[CH:]
                values = (bottom, top + pltpu.roll(bottom, CH, 1), pltpu.roll(top, CH, 1))
                for b in range(3):
                    spot = 9 * a + 3 * b + c
                    flat_k[spot * CH : (spot + 1) * CH, :] = values[b]
        evens = flat_k[pl.ds(0, K_ROWS, stride=2), :]
        odds = flat_k[pl.ds(1, K_ROWS, stride=2), :]
        wide = lax.broadcasted_iota(jnp.int32, (K_ROWS, ROW), 1)
        flat[layer * K_ROWS : (layer + 1) * K_ROWS, :] = jnp.where(
            wide < CH, evens, pltpu.roll(odds, CH, 1)
        )

    def centre(windows, offset):
        return jnp.concatenate(
            [windows[z + offset, ROW : 2 * ROW, :] for z in range(PLANES)], axis=1
        )

    kernel_grad(2, centre(wing3, 2), win2, 2)
    for pair in range(3):
        back = pair_product(backward_w[1], wing3, 2 * pair)
        for side in range(2):
            plane = 2 * pair + side - 1
            grad = slope2[plane + 1] * back[:, side * ROW : (side + 1) * ROW]
            grad = grad.astype(jnp.bfloat16).astype(jnp.float32)
            store_window(wing2, plane + 1, inside(plane, grad))
    kernel_grad(1, centre(wing2, 1), win1, 3)
    for pair in range(2):
        back = pair_product(backward_w[0], wing2, 2 * pair)
        for side in range(2):
            plane = 2 * pair + side
            grad = slope1[plane] * back[:, side * ROW : (side + 1) * ROW]
            grad1[:, plane * ROW : (plane + 1) * ROW] = grad.astype(jnp.bfloat16)
    kernel_grad(0, grad1[...], win0, 4)

    for block in range(SLABS):
        apart = block ^ slab
        piece = flat[block * ROWS : (block + 1) * ROWS, :]

        @pl.when((apart & 1) == 1)
        def _():
            send_ref[block // 2] = piece.astype(jnp.bfloat16)

        @pl.when((apart & 1) == 0)
        def _():
            keep_ref[block // 2] = piece


def local_step(slab, pieces, held, critic, critic_back, score):
    bf16, f32 = jnp.bfloat16, jnp.float32
    vmem = pl.BlockSpec(memory_space=pltpu.VMEM)
    return pl.pallas_call(
        local_kernel,
        out_shape=(
            jax.ShapeDtypeStruct((PLANES, CH, 2 * ROW), bf16),
            jax.ShapeDtypeStruct((SLABS // 2, ROWS, ROW), f32),
            jax.ShapeDtypeStruct((SLABS // 2, ROWS, ROW), bf16),
        ),
        in_specs=[pl.BlockSpec(memory_space=pltpu.SMEM)] + [vmem] * 9,
        out_specs=(vmem, vmem, vmem),
        scratch_shapes=[
            pltpu.VMEM((FLAT_ROWS, ROW), f32),
            pltpu.VMEM((2 * FLAT_ROWS, ROW), f32),
            pltpu.VMEM((3, ROW, 9 * ROW), bf16),
            pltpu.VMEM((2, ROW, 9 * ROW), bf16),
            pltpu.VMEM((14, 3 * ROW, ROW), bf16),
            pltpu.VMEM((12, 3 * ROW, ROW), bf16),
            pltpu.VMEM((10, 3 * ROW, ROW), bf16),
            pltpu.VMEM((8, 3 * ROW, ROW), bf16),
            pltpu.VMEM((6, 3 * ROW, ROW), bf16),
            pltpu.VMEM((ROW, PLANES * ROW), bf16),
            pltpu.VMEM((PLANES, ROW, ROW), f32),
            pltpu.VMEM((PLANES + 2, ROW, ROW), f32),
            pltpu.VMEM((2 * K_ROWS, ROW), f32),
            pltpu.VMEM((FLAT_ROWS, ROW), f32),
        ],
        compiler_params=pltpu.CompilerParams(vmem_limit_bytes=24 << 20),
        cost_estimate=pl.CostEstimate(
            flops=6_000_000_000, bytes_accessed=4_000_000, transcendentals=1_000_000
        ),
        name="local_step",
    )(slab, *pieces, held, critic, critic_back, score)


def move(value, axis, target_of):
    count = lax.axis_size(axis)
    return lax.ppermute(value, axis, [(i, target_of(i)) for i in range(count)])


def plane_exchange(slots):
    groups = [list(range(16)), list(range(16, 32))]
    return lax.all_to_all(slots, "trainer", 0, 0, axis_index_groups=groups)


def pack_kernel(weight_ref, moment_ref, out_ref, rows):
    rows[...] = jnp.zeros(rows.shape, jnp.float32)
    for index, source in enumerate((weight_ref, moment_ref)):
        for r in range(ROWS):
            spot = index * SECOND + r
            rows[spot : spot + 1, :] = source[:, r * ROW : (r + 1) * ROW]
    packed = rows[...].astype(jnp.bfloat16)
    for slot in range(16):
        out_ref[slot] = packed


def pack_slots(weight, moment):
    vmem = pl.BlockSpec(memory_space=pltpu.VMEM)
    return pl.pallas_call(
        pack_kernel,
        out_shape=(
            jax.ShapeDtypeStruct((16, 2 * SECOND, ROW), jnp.bfloat16),
            jax.ShapeDtypeStruct((2 * SECOND, ROW), jnp.float32),
        ),
        in_specs=[vmem, vmem],
        out_specs=(vmem, vmem),
        cost_estimate=pl.CostEstimate(flops=100_000, bytes_accessed=1_500_000, transcendentals=0),
        name="pack_slots",
    )(weight, moment)


def update_kernel(info, rows, held, moment_own, across, heard, weight_ref, moment_ref, fresh):
    grad = heard[0].astype(jnp.float32)
    for member in range(1, heard.shape[0]):
        grad = grad + heard[member].astype(jnp.float32)
    keeper = info[2] == 1
    far = lax.axis_index("depth") >> 3
    other_weight = held[far].astype(jnp.float32)
    other_moment = jnp.where(
        info[1] == 1, moment_own[...].astype(jnp.float32), across[...].astype(jnp.float32)
    )
    weight = jnp.where(keeper, rows[0:ROWS, :], other_weight)
    moment = jnp.where(keeper, rows[SECOND : SECOND + ROWS, :], other_moment)
    moment = momentum_decay * moment + grad
    fresh[0] = weight - step_length * moment
    fresh[1] = moment
    for index, target in enumerate((weight_ref, moment_ref)):
        for r in range(ROWS):
            target[:, r * ROW : (r + 1) * ROW] = fresh[index, r : r + 1, :]


def update(info, rows, held, moment_own, across, heard):
    vmem = pl.BlockSpec(memory_space=pltpu.VMEM)
    flat = jax.ShapeDtypeStruct((1, ROWS * ROW), jnp.float32)
    return pl.pallas_call(
        update_kernel,
        out_shape=(flat, flat),
        in_specs=[pl.BlockSpec(memory_space=pltpu.SMEM)] + [vmem] * 5,
        out_specs=(vmem, vmem),
        scratch_shapes=[pltpu.VMEM((2, ROWS, ROW), jnp.float32)],
        cost_estimate=pl.CostEstimate(flops=500_000, bytes_accessed=1_000_000, transcendentals=0),
        compiler_params=pltpu.CompilerParams(vmem_limit_bytes=8 << 20),
        name="update",
    )(info, rows, held, moment_own, across, heard)


def pick_kernel(
    pairing, flags, heard, slots, moment_own, moment_other, info, for_own, for_other, sems
):
    rank = lax.axis_index("trainer")
    half = rank >> 4
    across = rank ^ 16
    source = jnp.where(flags[rank] == 1, rank, pairing[rank])
    other = jnp.where(flags[across] == 1, across, pairing[across])
    first = pltpu.make_async_copy(heard.at[source & 15], for_own, sems.at[0])
    second = pltpu.make_async_copy(heard.at[other & 15], for_other, sems.at[1])
    first.start()
    second.start()
    info[0] = 2 * (source >> 4)
    info[1] = jnp.where((source >> 4) == half, 1, 0)
    info[2] = flags[rank]
    info[3] = half
    first.wait()
    second.wait()
    for member in range(4):
        slots[member] = jnp.where(half == member // 2, for_own[0:ROWS, :], for_other[0:ROWS, :])
    moment_own[...] = for_own[SECOND : SECOND + ROWS, :]
    moment_other[...] = for_other[SECOND : SECOND + ROWS, :]


def pick_slots(pairing, flags, heard):
    vmem = pl.BlockSpec(memory_space=pltpu.VMEM)
    smem = pl.BlockSpec(memory_space=pltpu.SMEM)
    share = jax.ShapeDtypeStruct((ROWS, ROW), jnp.bfloat16)
    return pl.pallas_call(
        pick_kernel,
        out_shape=(
            jax.ShapeDtypeStruct((4, ROWS, ROW), jnp.bfloat16),
            share,
            share,
            jax.ShapeDtypeStruct((4,), jnp.int32),
        ),
        in_specs=[smem, smem, pl.BlockSpec(memory_space=pl.ANY)],
        out_specs=(vmem, vmem, vmem, smem),
        scratch_shapes=[
            pltpu.VMEM((2 * SECOND, ROW), jnp.bfloat16),
            pltpu.VMEM((2 * SECOND, ROW), jnp.bfloat16),
            pltpu.SemaphoreType.DMA((2,)),
        ],
        cost_estimate=pl.CostEstimate(flops=100_000, bytes_accessed=400_000, transcendentals=0),
        compiler_params=pltpu.CompilerParams(vmem_limit_bytes=8 << 20),
        name="pick_slots",
    )(pairing, flags, heard)


def far_exchange(slots):
    depth = lax.axis_size("depth")
    groups = [
        [(t + s) * depth + d + e for s in (0, 16) for e in (0, 8)]
        for t in range(16)
        for d in range(8)
    ]
    return lax.all_to_all(slots, ("trainer", "depth"), 0, 0, axis_index_groups=groups)


def exchange_depth(keep, send):
    groups = [list(range(core, 16, 2)) for core in range(2)]
    mine = keep + move(send, "depth", lambda i: i ^ 1).astype(jnp.float32)
    return lax.all_to_all(
        mine.astype(jnp.bfloat16), "depth", 0, 0, axis_index_groups=groups
    )


def shifted(value, by):
    count = lax.axis_size("depth")
    links = [(i, i + by) for i in range(count) if 0 <= i + by < count]
    return lax.ppermute(value, "depth", links)


def critic_forms(disc):
    cube = disc.reshape(2, 2, 2, disc.shape[1], disc.shape[2])
    forward = cube.transpose(3, 0, 2, 1, 4).reshape(ROW, 8 * CH)
    backward = cube.transpose(0, 1, 4, 2, 3).reshape(4 * CH, 2 * ROW)
    return forward, backward


def one_step(noise, gen_weight, gen_momentum, disc_weight, score_weight, pairing, flags):
    together = lax.optimization_barrier
    slab = lax.axis_index("depth").astype(jnp.int32)
    latent = noise[0]
    packed, rows = pack_slots(gen_weight, gen_momentum)
    heard = plane_exchange(packed)
    pieces = (
        shifted(latent[PLANES - 1 :], 2),
        shifted(latent, 1),
        latent,
        shifted(latent, -1),
        shifted(latent[:1], -2),
    )
    critic, critic_back = critic_forms(disc_weight[0])
    score = jnp.broadcast_to(score_weight[0][:, None], (ROW, ROW))
    heard, pieces, critic, critic_back, score = together(
        (heard, pieces, critic, critic_back, score)
    )
    slots, moment_own, moment_other, info = pick_slots(pairing, flags, heard)
    got = far_exchange(slots)
    across = move(moment_other, "trainer", lambda i: i ^ 16)
    held = lax.dynamic_slice_in_dim(got, info[0], 2, 0)
    both = held
    near = [list(range(first, first + 8)) for first in range(0, 16, 8)]
    held = lax.all_gather(held, "depth", axis_index_groups=near)
    generated, keep, send = local_step(
        slab.reshape(1), pieces, held, critic, critic_back, score
    )
    keep, send, across = together((keep, send, across))
    new_weight, new_momentum = update(
        info, rows, both, moment_own, across, exchange_depth(keep, send)
    )
    return generated[None], new_weight, new_momentum


def solution(mesh):
    placed = (
        P("trainer", "depth", None, None),
        P("trainer", "depth"),
        P("trainer", "depth"),
        P("trainer", None, None, None),
        P("trainer", None),
        P(),
        P(),
    )
    return jax.shard_map(
        one_step,
        mesh=mesh,
        in_specs=placed,
        out_specs=(P("trainer", "depth", None, None), P("trainer", "depth"), P("trainer", "depth")),
        check_vma=False,
    )
```
